32 devices in a mesh: rows: 8 (over y, x, core), cols: 4 (over z).
Axes of the slice: x: 2, y: 2, z: 4, core: 2. Of those that a mesh axis runs over, the one named last changes fastest.
Arguments:
- snapshots: float32 [8192, 8192], P('rows', 'cols'), may hold values from -500 to 500, as said below
Outputs:
- updated: float32 [8192, 8192], P('rows', 'cols')
- coeffs: float32 [512, 8192], P(None, 'cols')
The draws below stay inside these ranges and needn't reach their ends.
Inputs may be any that keep to these rules, and one draw needn't show every extreme that they name: `snapshots`: Real-valued entries.
All inputs are finite; a program needn't handle non-finite values.
Results may differ from the reference program's by a relative error of at most 0.000055.
Values sent between devices are 32-bit elements; how exact they have to be, the bound alone decides.
No kernel may reach another device: no remote copies, remote signals or barrier semaphores. Data moves between devices by JAX's collectives and lax.ppermute only.
A program may use at most 128 MiB of HBM per device.

```python
import math
import jax
import jax.numpy as jnp
from jax import lax

SNAPS = 8192
PB = 512
ROWS = 8192


def draw_snapshots(key, part):
    key_base, key_col, key_row = jax.random.split(jax.random.fold_in(key, 17), 3)
    col_scale = jnp.exp(jax.random.uniform(key_col, (1, SNAPS), jnp.float32) * math.log(10.0))
    position = jnp.arange(ROWS, dtype=jnp.float32)[:, None] / ROWS
    row_scale = (1.0 + 2.0 * position) * jnp.exp(jax.random.uniform(key_row, (ROWS, 1), jnp.float32) * math.log(3.16))
    base = jnp.clip(jax.random.normal(key_base, (ROWS, SNAPS), jnp.float32), -5.0, 5.0)
    return base * row_scale * col_scale


def setup_inputs(seed: int = 0) -> dict:
    key_list = jax.random.split(jax.random.key(seed), 2)
    return {
        "snapshots": draw_snapshots(jax.random.fold_in(key_list[1], 71), 0),
    }


def reference(snapshots):
    highest = lax.Precision.HIGHEST
    panel = snapshots[:, :PB]
    gram = jnp.dot(panel.T.astype(jnp.float32), panel.astype(jnp.float32), precision=highest, preferred_element_type=jnp.float32) / ROWS
    lower = jnp.linalg.cholesky(gram)
    factor = lower.T
    basis = lax.linalg.triangular_solve(lower, panel, left_side=False, lower=True, transpose_a=True)
    proj = jnp.dot(basis.T.astype(jnp.float32), snapshots.astype(jnp.float32), precision=highest, preferred_element_type=jnp.float32) / ROWS
    column = jnp.arange(SNAPS, dtype=jnp.int32)
    is_panel = (column < PB)[None, :]
    filler = jnp.zeros((PB, SNAPS - PB), jnp.float32)
    coeffs = jnp.where(is_panel, jnp.concatenate([factor, filler], axis=1), proj)
    trailing = snapshots - jnp.dot(basis.astype(jnp.float32), proj.astype(jnp.float32), precision=highest, preferred_element_type=jnp.float32)
    padded = jnp.concatenate([basis, jnp.zeros((ROWS, SNAPS - PB), jnp.float32)], axis=1)
    updated = jnp.where(is_panel, padded, trailing)
    return (updated, coeffs)
```

```python
import jax
import jax.numpy as jnp
from jax import lax
from jax.experimental import pallas as pl
from jax.experimental.pallas import tpu as pltpu
from jax.sharding import PartitionSpec as P

PB = 512
NB = 128
CHUNKS = (256, 256)
F32 = jnp.float32
BF16 = jnp.bfloat16
HIGHEST = lax.Precision.HIGHEST
VMEM = pl.BlockSpec(memory_space=pltpu.VMEM)


def mm(a, b, da, db, precision=None):
    return lax.dot_general(
        a, b, (((da,), (db,)), ((), ())), precision=precision, preferred_element_type=F32
    )


def split(x):
    high = x.astype(BF16)
    return high, (x - high.astype(F32)).astype(BF16)


def diag_block(d_ref, z_ref, f_ref):
    a_all = d_ref[...]
    row = lax.broadcasted_iota(jnp.int32, (NB, NB), 0)
    col = lax.broadcasted_iota(jnp.int32, (NB, NB), 1)
    z_all = jnp.where(row == col, 1.0, 0.0).astype(F32)
    lane = lax.broadcasted_iota(jnp.int32, (1, NB), 1)
    for j in range(0, NB, 2):
        base = (j // 8) * 8
        if a_all.shape[0] != NB - base:
            a_all, z_all = a_all[8:], z_all[8:]
        i, n = j - base, NB - base
        r0, r1 = a_all[i : i + 1, :], a_all[i + 1 : i + 2, :]
        z0, z1 = z_all[i : i + 1, :], z_all[i + 1 : i + 2, :]
        c0 = jnp.broadcast_to(a_all[:, j : j + 1], (n, NB))
        c1 = jnp.broadcast_to(a_all[:, j + 1 : j + 2], (n, NB))
        a = jnp.broadcast_to(r0[:, j : j + 1], (1, NB))
        b = jnp.broadcast_to(r0[:, j + 1 : j + 2], (1, NB))
        d = jnp.broadcast_to(r1[:, j + 1 : j + 2], (1, NB))
        ra = 1.0 / a
        bra = b * ra
        s = d - b * bra
        rs = 1.0 / s
        t1 = r1 - bra * r0
        x1 = t1 * rs
        x0 = r0 * ra - bra * x1
        u1 = z1 - bra * z0
        y1 = u1 * rs
        y0 = z0 * ra - bra * y1
        qa, qs = lax.rsqrt(a), lax.rsqrt(s)
        f_ref[j : j + 1, :] = jnp.where(lane >= j, r0 * qa, 0.0)
        f_ref[j + 1 : j + 2, :] = jnp.where(lane >= j + 1, t1 * qs, 0.0)
        z_ref[j : j + 1, :] = z0 * qa
        z_ref[j + 1 : j + 2, :] = u1 * qs
        if j + 2 < NB:
            a_all = a_all - c0 * x0 - c1 * x1
            z_all = z_all - c0 * y0 - c1 * y1


def chol_kernel(g_ref, f_out, l_out, work, diag, zs, fs):
    n = g_ref.shape[0]
    nb = n // NB
    work[...] = g_ref[...]
    f_out[...] = jnp.zeros_like(f_out)
    l_out[...] = jnp.zeros_like(l_out)

    def body(k, carry):
        o = pl.multiple_of(k * NB, NB)
        diag[...] = work[pl.ds(o, NB), pl.ds(o, NB)]
        diag_block(diag, zs, fs)
        for kk in range(nb):

            @pl.when(k == kk)
            def _():
                o, e = kk * NB, kk * NB + NB
                z = zs[...]
                f_out[o:e, o:e] = fs[...]
                lk = z
                if kk > 0:
                    lk = jnp.concatenate([mm(z, l_out[o:e, :o], 1, 0, HIGHEST), z], axis=1)
                l_out[o:e, :e] = lk
                if kk < nb - 1:
                    u = mm(z, work[o:e, e:], 1, 0, HIGHEST)
                    f_out[o:e, e:] = u
                    work[e:, e:] -= mm(u, u, 0, 0, HIGHEST)
                    l_out[e:, :e] -= mm(u, lk, 0, 0, HIGHEST)

        return carry

    lax.fori_loop(0, nb, body, 0)


def chol_inv(gram):
    n = gram.shape[0]
    shape = jax.ShapeDtypeStruct((n, n), F32)
    return pl.pallas_call(
        chol_kernel,
        out_shape=(shape, shape),
        in_specs=[VMEM],
        out_specs=(VMEM, VMEM),
        scratch_shapes=[pltpu.VMEM((n, n), F32)] + [pltpu.VMEM((NB, NB), F32)] * 3,
        compiler_params=pltpu.CompilerParams(vmem_limit_bytes=16 << 20),
        cost_estimate=pl.CostEstimate(flops=10**10, bytes_accessed=3 << 20, transcendentals=0),
        name="chol_inv",
    )(gram)


def finish(info, snapshots, panel, linv, factor, pieces, layout):
    rows, cols = snapshots.shape
    tile = 256
    n_pieces = len(pieces)

    def kernel(info_ref, s_ref, p_ref, l_ref, f_ref, *rest):
        m_refs = rest[:n_pieces]
        up_ref, co_ref, bs, b3, l3, ms, m3, p3 = rest[n_pieces:]
        j = pl.program_id(0)

        @pl.when(j == 0)
        def _():
            lh, ll = split(l_ref[...])
            l3[:, :PB], l3[:, PB : 2 * PB], l3[:, 2 * PB :] = lh, lh, ll
            for r in range(0, rows, 256):
                ph, plow = split(p_ref[r : r + 256, :])
                b = mm(ph, lh, 1, 1) + (mm(ph, ll, 1, 1) + mm(plow, lh, 1, 1))
                bs[r : r + 256, :] = b
                bh, bl = split(b)
                b3[r : r + 256, :PB], b3[r : r + 256, PB : 2 * PB] = bh, bh
                b3[r : r + 256, 2 * PB :] = bl

        for ref, (base, core, chip) in zip(m_refs, layout):
            h = ref.shape[0]
            off = base + (info_ref[1] ^ core) * (h * (n_chips(layout))) + (info_ref[2] ^ chip) * h
            ms[pl.ds(pl.multiple_of(off, 8), h), :] = ref[...]
        mh, ml = split(ms[...])
        m3[:PB, :], m3[PB : 2 * PB, :], m3[2 * PB :, :] = mh, ml, mh
        proj = mm(l3[...], m3[...], 1, 0)
        ph, plow = split(proj)
        p3[:PB, :], p3[PB : 2 * PB, :], p3[2 * PB :, :] = ph, plow, ph
        co_ref[...] = proj
        for r in range(0, rows, 256):
            up_ref[r : r + 256, :] = s_ref[r : r + 256, :] - mm(b3[r : r + 256, :], p3[...], 1, 0)
        for t in range(PB // tile):

            @pl.when((info_ref[0] == 0) & (j == t))
            def _():
                co_ref[...] = f_ref[:, t * tile : (t + 1) * tile]
                up_ref[...] = bs[:, t * tile : (t + 1) * tile]

    full = lambda a: pl.BlockSpec(a.shape, lambda j, *_: (0, 0), pipeline_mode=pl.Buffered(1))
    col = lambda h: pl.BlockSpec((h, tile), lambda j, *_: (0, j))
    return pl.pallas_call(
        kernel,
        out_shape=(
            jax.ShapeDtypeStruct((rows, cols), F32),
            jax.ShapeDtypeStruct((PB, cols), F32),
        ),
        grid_spec=pltpu.PrefetchScalarGridSpec(
            num_scalar_prefetch=1,
            grid=(cols // tile,),
            in_specs=[col(rows), full(panel), full(linv), full(factor)]
            + [col(p.shape[0]) for p in pieces],
            out_specs=(col(rows), col(PB)),
            scratch_shapes=[
                pltpu.VMEM((rows, PB), F32),
                pltpu.VMEM((rows, 3 * PB), BF16),
                pltpu.VMEM((PB, 3 * PB), BF16),
                pltpu.VMEM((PB, tile), F32),
                pltpu.VMEM((3 * PB, tile), BF16),
                pltpu.VMEM((3 * PB, tile), BF16),
            ],
        ),
        compiler_params=pltpu.CompilerParams(vmem_limit_bytes=40 << 20),
        name="finish",
    )(info, snapshots, panel, linv, factor, *pieces)


def n_chips(layout):
    return 1 + max(chip for _, _, chip in layout)


def spread(x, n):
    if n == 1:
        return x
    rows = x.shape[0]
    parts = n - 1
    size = -(-rows // (8 * parts)) * 8
    starts = [min(k * size, rows - size) for k in range(parts)]
    z = lax.axis_index("cols")
    mine = None
    for k in range(parts):
        part = lax.ppermute(x[starts[k] : starts[k] + size], "cols", [(0, k + 1)])
        mine = part if mine is None else mine + part
    out = jnp.where(z == 0, x, 0.0)
    table = jnp.array(starts, jnp.int32)

    def place(out, part, owner):
        start = jnp.minimum(owner * size, rows - size)
        old = lax.dynamic_slice(out, (start, 0), part.shape)
        return lax.dynamic_update_slice(out, jnp.where(z == 0, old, part), (start, 0))

    out = place(out, mine, jnp.maximum(z - 1, 0))
    for k in range(1, parts):
        got = lax.ppermute(mine, "cols", [(1 + i, 1 + (i + k) % parts) for i in range(parts)])
        out = place(out, got, jnp.maximum(z - 1 - k, 0) + jnp.where(z - 1 - k < 0, parts + z - 1 - k, 0))
    return out


def reduce_rows(m, n):
    index = lax.axis_index("rows")
    core, chip = index & 1, index >> 1
    chips, half = n // 2, m.shape[0] // 2
    piece = half // chips
    swap = lambda k: [(i, i ^ k) for i in range(n)]
    take = lambda a, start, size: lax.dynamic_slice_in_dim(a, start, size, 0)
    other = lax.ppermute(take(m, (1 - core) * half, half), "rows", swap(1))
    mine = take(m, core * half, half) + other
    own = take(mine, chip * piece, piece)
    for k in range(1, chips):
        own = own + lax.ppermute(take(mine, (chip ^ k) * piece, piece), "rows", swap(2 * k))
    got = [own] + [lax.ppermute(own, "rows", swap(2 * k)) for k in range(1, chips)]
    pieces = [(g, 0, k) for k, g in enumerate(got)]
    pieces += [(lax.ppermute(g, "rows", swap(1)), 1, k) for k, g in enumerate(got)]
    return pieces


def shards(snapshots):
    rows_dev, cols_dev = snapshots.shape
    n_rows, n_cols = lax.axis_size("rows"), lax.axis_size("cols")
    total_rows = rows_dev * n_rows
    z = lax.axis_index("cols")
    index = lax.axis_index("rows")
    panel = snapshots[:, :PB]
    gram = mm(panel, panel, 0, 0, HIGHEST) / total_rows
    gram = lax.psum(jnp.where(z == 0, gram, 0.0), ("rows", "cols"))
    panels, pieces, layout = [], [], []
    base = 0
    for width in CHUNKS:
        part = spread(panel[:, base : base + width], n_cols)
        panels.append(part)
        m = mm(part, snapshots, 0, 0, lax.Precision.HIGH) / total_rows
        for piece, core, chip in reduce_rows(m, n_rows):
            pieces.append(piece)
            layout.append((base, core, chip))
        base += width
    factor, linv = chol_inv(gram)
    info = jnp.stack([z, index & 1, index >> 1]).astype(jnp.int32)
    panel = jnp.concatenate(panels, axis=1)
    return finish(info, snapshots, panel, linv, factor, pieces, layout)


def solution(mesh):
    in_specs = (P("rows", "cols"),)
    out_specs = (P("rows", "cols"), P(None, "cols"))
    return jax.shard_map(shards, mesh=mesh, in_specs=in_specs, out_specs=out_specs, check_vma=False)
```

```python
import jax
import jax.numpy as jnp
from jax import lax
from jax.experimental import pallas as pl
from jax.experimental.pallas import tpu as pltpu
from jax.sharding import PartitionSpec as P

PB = 512
NB = 128
F32 = jnp.float32
BF16 = jnp.bfloat16
HIGHEST = lax.Precision.HIGHEST
VMEM = pl.BlockSpec(memory_space=pltpu.VMEM)


def mm(a, b, da, db, precision=None):
    return lax.dot_general(
        a, b, (((da,), (db,)), ((), ())), precision=precision, preferred_element_type=F32
    )


def split(x):
    high = x.astype(BF16)
    return high, (x - high.astype(F32)).astype(BF16)


def diag_block(d_ref, z_ref, f_ref):
    a_all = d_ref[...]
    row = lax.broadcasted_iota(jnp.int32, (NB, NB), 0)
    col = lax.broadcasted_iota(jnp.int32, (NB, NB), 1)
    z_all = jnp.where(row == col, 1.0, 0.0).astype(F32)
    lane = lax.broadcasted_iota(jnp.int32, (1, NB), 1)
    for j in range(0, NB, 2):
        base = (j // 8) * 8
        if a_all.shape[0] != NB - base:
            a_all, z_all = a_all[8:], z_all[8:]
        i, n = j - base, NB - base
        r0, r1 = a_all[i : i + 1, :], a_all[i + 1 : i + 2, :]
        z0, z1 = z_all[i : i + 1, :], z_all[i + 1 : i + 2, :]
        c0 = jnp.broadcast_to(a_all[:, j : j + 1], (n, NB))
        c1 = jnp.broadcast_to(a_all[:, j + 1 : j + 2], (n, NB))
        a = jnp.broadcast_to(r0[:, j : j + 1], (1, NB))
        b = jnp.broadcast_to(r0[:, j + 1 : j + 2], (1, NB))
        d = jnp.broadcast_to(r1[:, j + 1 : j + 2], (1, NB))
        ra = 1.0 / a
        bra = b * ra
        s = d - b * bra
        rs = 1.0 / s
        t1 = r1 - bra * r0
        x1 = t1 * rs
        x0 = r0 * ra - bra * x1
        u1 = z1 - bra * z0
        y1 = u1 * rs
        y0 = z0 * ra - bra * y1
        qa, qs = lax.rsqrt(a), lax.rsqrt(s)
        f_ref[j : j + 1, :] = jnp.where(lane >= j, r0 * qa, 0.0)
        f_ref[j + 1 : j + 2, :] = jnp.where(lane >= j + 1, t1 * qs, 0.0)
        z_ref[j : j + 1, :] = z0 * qa
        z_ref[j + 1 : j + 2, :] = u1 * qs
        if j + 2 < NB:
            a_all = a_all - c0 * x0 - c1 * x1
            z_all = z_all - c0 * y0 - c1 * y1


def chol_part(info, first, last, pieces=None, places=None, state=None):
    fresh = pieces is not None
    arrays = pieces if fresh else state
    n = arrays[0].shape[1]
    nb = n // NB
    n_in = len(arrays)

    def kernel(info_ref, *refs):
        work, f_out, l_out = refs[n_in : n_in + 3]
        diag, zs, fs = refs[n_in + 3 :]
        if fresh:
            chips = n_in // 2
            for ref, (core, chip) in zip(refs, places):
                h = ref.shape[0]
                off = (info_ref[1] ^ core) * (h * chips) + (info_ref[2] ^ chip) * h
                work[pl.ds(pl.multiple_of(off, 8), h), :] = ref[...]
            f_out[...] = jnp.zeros_like(f_out)
            l_out[...] = jnp.zeros_like(l_out)

        def body(k, carry):
            o = pl.multiple_of(k * NB, NB)
            diag[...] = work[pl.ds(o, NB), pl.ds(o, NB)]
            diag_block(diag, zs, fs)
            for kk in range(first, last):

                @pl.when(k == kk)
                def _():
                    o, e = kk * NB, kk * NB + NB
                    z = zs[...]
                    f_out[o:e, o:e] = fs[...]
                    lk = z
                    if kk > 0:
                        lk = jnp.concatenate([mm(z, l_out[o:e, :o], 1, 0, HIGHEST), z], axis=1)
                    l_out[o:e, :e] = lk
                    if kk < nb - 1:
                        u = mm(z, work[o:e, e:], 1, 0, HIGHEST)
                        f_out[o:e, e:] = u
                        work[e:, e:] -= mm(u, u, 0, 0, HIGHEST)
                        l_out[e:, :e] -= mm(u, lk, 0, 0, HIGHEST)

            return carry

        lax.fori_loop(first, last, body, 0)

    shape = jax.ShapeDtypeStruct((n, n), F32)
    return pl.pallas_call(
        kernel,
        out_shape=(shape, shape, shape),
        in_specs=[pl.BlockSpec(memory_space=pltpu.SMEM)] + [VMEM] * n_in,
        out_specs=(VMEM, VMEM, VMEM),
        scratch_shapes=[pltpu.VMEM((NB, NB), F32)] * 3,
        input_output_aliases={} if fresh else {1: 0, 2: 1, 3: 2},
        compiler_params=pltpu.CompilerParams(vmem_limit_bytes=16 << 20),
        cost_estimate=pl.CostEstimate(
            flops=(last - first) * 8 * 10**9, bytes_accessed=3 << 20, transcendentals=0
        ),
        name="chol_part",
    )(info, *arrays)


def finish(info, snapshots, panels, linv, factor, pieces, layout, tile=256, block=1024):
    rows, cols = snapshots.shape
    n_pieces, n_panels = len(pieces), len(panels)
    chips = 1 + max(chip for _, _, chip in layout)
    bases = [sum(p.shape[1] for p in panels[:i]) for i in range(n_panels)]

    def kernel(info_ref, s_ref, l_ref, f_ref, *rest):
        p_refs, rest = rest[:n_panels], rest[n_panels:]
        m_refs = rest[:n_pieces]
        up_ref, co_ref, bs, b3, l3, ms, m3, p3 = rest[n_pieces:]
        j = pl.program_id(0)

        @pl.when(j == 0)
        def _():
            lh, ll = split(l_ref[...])
            l3[:, :PB], l3[:, PB : 2 * PB], l3[:, 2 * PB :] = lh, lh, ll
            for r in range(0, rows, 256):
                b = 0.0
                for base, p_ref in zip(bases, p_refs):
                    end = base + p_ref.shape[1]
                    ph, plow = split(p_ref[r : r + 256, :])
                    lhs = jnp.concatenate([ph, ph, plow], axis=1)
                    rhs = jnp.concatenate([lh[:, base:end], ll[:, base:end], lh[:, base:end]], axis=1)
                    b = b + mm(lhs, rhs, 1, 1)
                bs[r : r + 256, :] = b
                bh, bl = split(b)
                b3[r : r + 256, :PB], b3[r : r + 256, PB : 2 * PB] = bh, bh
                b3[r : r + 256, 2 * PB :] = bl

        for ref, (base, core, chip) in zip(m_refs, layout):
            h = ref.shape[0]
            off = base + (info_ref[1] ^ core) * (h * chips) + (info_ref[2] ^ chip) * h
            ms[pl.ds(pl.multiple_of(off, 8), h), :] = ref[...]
        mh, ml = split(ms[...])
        m3[:PB, :], m3[PB : 2 * PB, :], m3[2 * PB :, :] = mh, ml, mh
        proj = mm(l3[...], m3[...], 1, 0)
        ph, plow = split(proj)
        p3[:PB, :], p3[PB : 2 * PB, :], p3[2 * PB :, :] = ph, plow, ph
        co_ref[...] = proj
        for r in range(0, rows, block):
            up_ref[r : r + block, :] = s_ref[r : r + block, :] - mm(b3[r : r + block, :], p3[...], 1, 0)
        for t in range(PB // tile):

            @pl.when((info_ref[0] == 0) & (j == t))
            def _():
                co_ref[...] = f_ref[:, t * tile : (t + 1) * tile]
                up_ref[...] = bs[:, t * tile : (t + 1) * tile]

    full = lambda a: pl.BlockSpec(a.shape, lambda j, *_: (0, 0), pipeline_mode=pl.Buffered(1))
    col = lambda h: pl.BlockSpec((h, tile), lambda j, *_: (0, j))
    return pl.pallas_call(
        kernel,
        out_shape=(
            jax.ShapeDtypeStruct((rows, cols), F32),
            jax.ShapeDtypeStruct((PB, cols), F32),
        ),
        grid_spec=pltpu.PrefetchScalarGridSpec(
            num_scalar_prefetch=1,
            grid=(cols // tile,),
            in_specs=[col(rows), full(linv), full(factor)]
            + [full(p) for p in panels]
            + [col(p.shape[0]) for p in pieces],
            out_specs=(col(rows), col(PB)),
            scratch_shapes=[
                pltpu.VMEM((rows, PB), F32),
                pltpu.VMEM((rows, 3 * PB), BF16),
                pltpu.VMEM((PB, 3 * PB), BF16),
                pltpu.VMEM((PB, tile), F32),
                pltpu.VMEM((3 * PB, tile), BF16),
                pltpu.VMEM((3 * PB, tile), BF16),
            ],
        ),
        compiler_params=pltpu.CompilerParams(vmem_limit_bytes=58 << 20),
        cost_estimate=pl.CostEstimate(
            flops=6 * PB * cols * (rows + PB), bytes_accessed=8 * rows * cols, transcendentals=0
        ),
        name="finish",
    )(info, snapshots, linv, factor, *panels, *pieces)


def panel_dot(info, snapshots, parts, size, base, width, scale, tile=256):
    rows, cols = snapshots.shape
    half = width // 2
    n_parts = len(parts)

    def kernel(info_ref, s_ref, own_ref, *rest):
        part_refs = rest[:n_parts]
        send_ref, mine_ref, p_ref, pt3, s3, ms = rest[n_parts:]
        j = pl.program_id(0)

        @pl.when((j == 0) & (info_ref[0] == 0))
        def _():
            p_ref[...] = own_ref[...]

        if n_parts:

            @pl.when((j == 0) & (info_ref[0] != 0))
            def _():
                for k, ref in enumerate(part_refs):
                    start = pl.multiple_of(info_ref[3 + k], 8)
                    p_ref[pl.ds(start, size), :] = ref[...]

        @pl.when(j == 0)
        def _():
            for r in range(0, rows, 256):
                ph, plow = split(p_ref[r : r + 256, :])
                pt = ph.T
                pt3[:, r : r + 256], pt3[:, rows + r : rows + r + 256] = pt, pt
                pt3[:, 2 * rows + r : 2 * rows + r + 256] = plow.T

        sh, sl = split(s_ref[...])
        s3[:rows, :], s3[rows : 2 * rows, :], s3[2 * rows :, :] = sh, sl, sh
        ms[...] = mm(pt3[...], s3[...], 1, 0) * scale
        send_ref[...] = ms[pl.ds(pl.multiple_of((1 - info_ref[1]) * half, half), half), :]
        mine_ref[...] = ms[pl.ds(pl.multiple_of(info_ref[1] * half, half), half), :]

    full = lambda a: pl.BlockSpec(a.shape, lambda j, *_: (0, 0), pipeline_mode=pl.Buffered(1))
    col = lambda h: pl.BlockSpec((h, tile), lambda j, *_: (0, j))
    out = jax.ShapeDtypeStruct((half, cols), F32)
    return pl.pallas_call(
        kernel,
        out_shape=(out, out, jax.ShapeDtypeStruct((rows, width), F32)),
        grid_spec=pltpu.PrefetchScalarGridSpec(
            num_scalar_prefetch=1,
            grid=(cols // tile,),
            in_specs=[
                col(rows),
                pl.BlockSpec(
                    (rows, width), lambda j, *_: (0, base // width), pipeline_mode=pl.Buffered(1)
                ),
            ]
            + [full(p) for p in parts],
            out_specs=(col(half), col(half), pl.BlockSpec((rows, width), lambda j, *_: (0, 0))),
            scratch_shapes=[
                pltpu.VMEM((width, 3 * rows), BF16),
                pltpu.VMEM((3 * rows, tile), BF16),
                pltpu.VMEM((width, tile), F32),
            ],
        ),
        compiler_params=pltpu.CompilerParams(vmem_limit_bytes=58 << 20),
        cost_estimate=pl.CostEstimate(
            flops=6 * rows * cols * width, bytes_accessed=4 * rows * cols, transcendentals=0
        ),
        name="panel_dot",
    )(info, snapshots, snapshots, *parts)


def part_size(rows, parts):
    return -(-rows // (8 * parts)) * 8


def spread_out(x, n):
    rows, parts = x.shape[0], n - 1
    size = part_size(rows, parts)
    mine = None
    for k in reversed(range(parts)):
        start = min(k * size, rows - size)
        part = lax.ppermute(x[start : start + size], "cols", [(0, k + 1)])
        mine = part if mine is None else mine + part
    return mine


def spread_round(mine, n):
    got, parts = [mine], n - 1
    for k in range(1, parts):
        pairs = [(1 + i, 1 + (i + k) % parts) for i in range(parts)]
        got.append(lax.ppermute(mine, "cols", pairs))
    return got


def after(x, *others):
    return lax.optimization_barrier((x, others))[0]


def swap(n, k):
    return [(i, i ^ k) for i in range(n)]


def take(a, start, size):
    return lax.dynamic_slice_in_dim(a, start, size, 0)


def join_cores(send, mine, n):
    return mine + lax.ppermute(send, "rows", swap(n, 1))


def scatter_chips(mine, n):
    chips = n // 2
    chip = lax.axis_index("rows") >> 1
    piece = mine.shape[0] // chips
    own = take(mine, chip * piece, piece)
    for k in range(1, chips):
        own = own + lax.ppermute(take(mine, (chip ^ k) * piece, piece), "rows", swap(n, 2 * k))
    return own


def gather_rows(own, n):
    got = [own] + [lax.ppermute(own, "rows", swap(n, 2 * k)) for k in range(1, n // 2)]
    other = [lax.ppermute(g, "rows", swap(n, 1)) for g in got]
    return got + other, [(0, k) for k in range(n // 2)] + [(1, k) for k in range(n // 2)]


def shards(snapshots):
    rows_dev, cols_dev = snapshots.shape
    n_rows, n_cols = lax.axis_size("rows"), lax.axis_size("cols")
    total_rows = rows_dev * n_rows
    z, index = lax.axis_index("cols"), lax.axis_index("rows")
    core = index & 1
    parts = n_cols - 1
    size = part_size(rows_dev, parts)
    starts = [jnp.minimum(((z - 1 - k) % parts) * size, rows_dev - size) for k in range(parts)]
    info = jnp.stack([z, core, index >> 1] + starts).astype(jnp.int32)
    half = PB // 2
    panel = snapshots[:, :PB]
    dot = lambda got, base: panel_dot(
        info, snapshots, got, size, base, half, 1.0 / total_rows
    )

    mine_a = spread_out(panel[:, :half], n_cols)
    gram = mm(panel, panel, 0, 0, HIGHEST) / total_rows
    joined = join_cores(take(gram, (1 - core) * half, half), take(gram, core * half, half), n_rows)
    share = scatter_chips(joined, n_rows)
    far = [lax.ppermute(share, "cols", [(0, k)]) for k in reversed(range(1, n_cols))]
    share = jnp.where(z == 0, share, sum(far, jnp.zeros_like(share)))
    grams, places = gather_rows(share, n_rows)

    got_a = spread_round(mine_a, n_cols)
    mine_b = spread_out(after(panel[:, half:], mine_a, share), n_cols)
    send, keep, panel_a = dot(got_a, 0)
    grams = after(grams, send)
    state = chol_part(info, 0, 1, pieces=grams, places=places)
    joined = join_cores(send, keep, n_rows)
    own_a = scatter_chips(joined, n_rows)
    got_b = spread_round(mine_b, n_cols)
    state = chol_part(info, 1, 2, state=after(state, joined, mine_b))
    pieces_a, where = gather_rows(own_a, n_rows)
    send, keep, panel_b = dot(after(got_b, own_a), half)
    joined = join_cores(send, keep, n_rows)
    own_b = scatter_chips(joined, n_rows)
    state = chol_part(info, 2, 3, state=after(state, joined))
    pieces_b, _ = gather_rows(own_b, n_rows)
    _, factor, linv = chol_part(info, 3, 4, state=after(state, own_b))
    layout = [(base,) + w for base in (0, half) for w in where]
    return finish(
        info, snapshots, [panel_a, panel_b], linv, factor, pieces_a + pieces_b, layout
    )


def solution(mesh):
    in_specs = (P("rows", "cols"),)
    out_specs = (P("rows", "cols"), P(None, "cols"))
    return jax.shard_map(shards, mesh=mesh, in_specs=in_specs, out_specs=out_specs, check_vma=False)
```

```python
import jax
import jax.numpy as jnp
from jax import lax
from jax.experimental import pallas as pl
from jax.experimental.pallas import tpu as pltpu
from jax.sharding import PartitionSpec as P

PB = 512
NB = 128
MERGE_COST = 3 * 10**10
F32 = jnp.float32
BF16 = jnp.bfloat16
HIGHEST = lax.Precision.HIGHEST
VMEM = pl.BlockSpec(memory_space=pltpu.VMEM)


def mm(a, b, da, db, precision=None):
    return lax.dot_general(
        a, b, (((da,), (db,)), ((), ())), precision=precision, preferred_element_type=F32
    )


def split(x):
    high = x.astype(BF16)
    return high, (x - high.astype(F32)).astype(BF16)


def diag_block(d_ref, z_ref, f_ref):
    a_all = d_ref[...]
    row = lax.broadcasted_iota(jnp.int32, (NB, NB), 0)
    col = lax.broadcasted_iota(jnp.int32, (NB, NB), 1)
    z_all = jnp.where(row == col, 1.0, 0.0).astype(F32)
    lane = lax.broadcasted_iota(jnp.int32, (1, NB), 1)
    for j in range(0, NB, 2):
        base = (j // 8) * 8
        if a_all.shape[0] != NB - base:
            a_all, z_all = a_all[8:], z_all[8:]
        i, n = j - base, NB - base
        r0, r1 = a_all[i : i + 1, :], a_all[i + 1 : i + 2, :]
        z0, z1 = z_all[i : i + 1, :], z_all[i + 1 : i + 2, :]
        c0 = jnp.broadcast_to(a_all[:, j : j + 1], (n, NB))
        c1 = jnp.broadcast_to(a_all[:, j + 1 : j + 2], (n, NB))
        a = jnp.broadcast_to(r0[:, j : j + 1], (1, NB))
        b = jnp.broadcast_to(r0[:, j + 1 : j + 2], (1, NB))
        d = jnp.broadcast_to(r1[:, j + 1 : j + 2], (1, NB))
        ra = 1.0 / a
        bra = b * ra
        s = d - b * bra
        rs = 1.0 / s
        t1 = r1 - bra * r0
        x1 = t1 * rs
        x0 = r0 * ra - bra * x1
        u1 = z1 - bra * z0
        y1 = u1 * rs
        y0 = z0 * ra - bra * y1
        qa, qs = lax.rsqrt(a), lax.rsqrt(s)
        f_ref[j : j + 1, :] = jnp.where(lane >= j, r0 * qa, 0.0)
        f_ref[j + 1 : j + 2, :] = jnp.where(lane >= j + 1, t1 * qs, 0.0)
        z_ref[j : j + 1, :] = z0 * qa
        z_ref[j + 1 : j + 2, :] = u1 * qs
        if j + 2 < NB:
            a_all = a_all - c0 * x0 - c1 * x1
            z_all = z_all - c0 * y0 - c1 * y1


def chol_part(info, first, last, pieces=None, places=None, state=None):
    fresh = pieces is not None
    arrays = pieces if fresh else state
    n = arrays[0].shape[1]
    nb = n // NB
    n_in = len(arrays)

    def kernel(info_ref, *refs):
        work, f_out, l_out = refs[n_in : n_in + 3]
        diag, zs, fs = refs[n_in + 3 :]
        if fresh:
            chips = n_in // 2
            for ref, (core, chip) in zip(refs, places):
                h = ref.shape[0]
                off = (info_ref[1] ^ core) * (h * chips) + (info_ref[2] ^ chip) * h
                work[pl.ds(pl.multiple_of(off, 8), h), :] = ref[...]
            f_out[...] = jnp.zeros_like(f_out)
            l_out[...] = jnp.zeros_like(l_out)

        def body(k, carry):
            o = pl.multiple_of(k * NB, NB)
            diag[...] = work[pl.ds(o, NB), pl.ds(o, NB)]
            diag_block(diag, zs, fs)
            for kk in range(first, last):

                @pl.when(k == kk)
                def _():
                    o, e = kk * NB, kk * NB + NB
                    z = zs[...]
                    f_out[o:e, o:e] = fs[...]
                    lk = z
                    if kk > 0:
                        lk = jnp.concatenate([mm(z, l_out[o:e, :o], 1, 0, HIGHEST), z], axis=1)
                    l_out[o:e, :e] = lk
                    if kk < nb - 1:
                        u = mm(z, work[o:e, e:], 1, 0, HIGHEST)
                        f_out[o:e, e:] = u
                        work[e:, e:] -= mm(u, u, 0, 0, HIGHEST)
                        l_out[e:, :e] -= mm(u, lk, 0, 0, HIGHEST)

            return carry

        lax.fori_loop(first, last, body, 0)

    shape = jax.ShapeDtypeStruct((n, n), F32)
    return pl.pallas_call(
        kernel,
        out_shape=(shape, shape, shape),
        in_specs=[pl.BlockSpec(memory_space=pltpu.SMEM)] + [VMEM] * n_in,
        out_specs=(VMEM, VMEM, VMEM),
        scratch_shapes=[pltpu.VMEM((NB, NB), F32)] * 3,
        input_output_aliases={} if fresh else {1: 0, 2: 1, 3: 2},
        compiler_params=pltpu.CompilerParams(vmem_limit_bytes=16 << 20),
        cost_estimate=pl.CostEstimate(
            flops=(last - first) * 8 * 10**9, bytes_accessed=3 << 20, transcendentals=0
        ),
        name="chol_part",
    )(info, *arrays)


def finish(info, snapshots, panels, linv, factor, pieces, layout, tile=512):
    rows, cols = snapshots.shape
    n_pieces, n_panels = len(pieces), len(panels)
    chips = 1 + max(chip for _, _, chip in layout)
    bases = [sum(p.shape[1] for p in panels[:i]) for i in range(n_panels)]

    def kernel(info_ref, s_ref, l_ref, f_ref, *rest):
        p_refs, rest = rest[:n_panels], rest[n_panels:]
        m_refs = rest[:n_pieces]
        up_ref, co_ref, bs, b3, l3, ms, m3, p3 = rest[n_pieces:]
        j = pl.program_id(0)

        @pl.when(j == 0)
        def _():
            lh, ll = split(l_ref[...])
            l3[:, :PB], l3[:, PB : 2 * PB], l3[:, 2 * PB :] = lh, lh, ll
            for r in range(0, rows, 256):
                b = 0.0
                for base, p_ref in zip(bases, p_refs):
                    end = base + p_ref.shape[1]
                    ph, plow = split(p_ref[r : r + 256, :])
                    lhs = jnp.concatenate([ph, ph, plow], axis=1)
                    rhs = jnp.concatenate([lh[:, base:end], ll[:, base:end], lh[:, base:end]], axis=1)
                    b = b + mm(lhs, rhs, 1, 1)
                bs[r : r + 256, :] = b
                bh, bl = split(b)
                b3[r : r + 256, :PB], b3[r : r + 256, PB : 2 * PB] = bh, bh
                b3[r : r + 256, 2 * PB :] = bl

        for ref, (base, core, chip) in zip(m_refs, layout):
            h = ref.shape[0]
            off = base + (info_ref[1] ^ core) * (h * chips) + (info_ref[2] ^ chip) * h
            ms[pl.ds(pl.multiple_of(off, 8), h), :] = ref[...]
        mh, ml = split(ms[...])
        m3[:PB, :], m3[PB : 2 * PB, :], m3[2 * PB :, :] = mh, ml, mh
        proj = mm(l3[...], m3[...], 1, 0)
        ph, plow = split(proj)
        p3[:PB, :], p3[PB : 2 * PB, :], p3[2 * PB :, :] = ph, plow, ph
        co_ref[...] = proj
        up_ref[...] = s_ref[...] - mm(b3[...], p3[...], 1, 0)
        for t in range(PB // tile):

            @pl.when((info_ref[0] == 0) & (j == t))
            def _():
                co_ref[...] = f_ref[:, t * tile : (t + 1) * tile]
                up_ref[...] = bs[:, t * tile : (t + 1) * tile]

    full = lambda a: pl.BlockSpec(a.shape, lambda j, *_: (0, 0), pipeline_mode=pl.Buffered(1))
    col = lambda h: pl.BlockSpec((h, tile), lambda j, *_: (0, j))
    return pl.pallas_call(
        kernel,
        out_shape=(
            jax.ShapeDtypeStruct((rows, cols), F32),
            jax.ShapeDtypeStruct((PB, cols), F32),
        ),
        grid_spec=pltpu.PrefetchScalarGridSpec(
            num_scalar_prefetch=1,
            grid=(cols // tile,),
            in_specs=[col(rows), full(linv), full(factor)]
            + [full(p) for p in panels]
            + [col(p.shape[0]) for p in pieces],
            out_specs=(col(rows), col(PB)),
            scratch_shapes=[
                pltpu.VMEM((rows, PB), F32),
                pltpu.VMEM((rows, 3 * PB), BF16),
                pltpu.VMEM((PB, 3 * PB), BF16),
                pltpu.VMEM((PB, tile), F32),
                pltpu.VMEM((3 * PB, tile), BF16),
                pltpu.VMEM((3 * PB, tile), BF16),
            ],
        ),
        compiler_params=pltpu.CompilerParams(vmem_limit_bytes=58 << 20),
        cost_estimate=pl.CostEstimate(
            flops=6 * PB * cols * (rows + PB), bytes_accessed=8 * rows * cols, transcendentals=0
        ),
        name="finish",
    )(info, snapshots, linv, factor, *panels, *pieces)


def panel_dot(info, snapshots, parts, size, base, width, scale, tile=512):
    rows, cols = snapshots.shape
    half = width // 2
    n_parts = len(parts)

    def kernel(info_ref, s_ref, own_ref, *rest):
        part_refs = rest[:n_parts]
        send_ref, mine_ref, p_ref, pt3, s3, ms = rest[n_parts:]
        j = pl.program_id(0)

        @pl.when((j == 0) & (info_ref[0] == 0))
        def _():
            p_ref[...] = own_ref[...]

        if n_parts:

            @pl.when((j == 0) & (info_ref[0] != 0))
            def _():
                for k, ref in enumerate(part_refs):
                    start = pl.multiple_of(info_ref[3 + k], 8)
                    p_ref[pl.ds(start, size), :] = ref[...]

        @pl.when(j == 0)
        def _():
            for r in range(0, rows, 256):
                ph, plow = split(p_ref[r : r + 256, :])
                pt = ph.T
                pt3[:, r : r + 256], pt3[:, rows + r : rows + r + 256] = pt, pt
                pt3[:, 2 * rows + r : 2 * rows + r + 256] = plow.T

        sh, sl = split(s_ref[...])
        s3[:rows, :], s3[rows : 2 * rows, :], s3[2 * rows :, :] = sh, sl, sh
        ms[...] = mm(pt3[...], s3[...], 1, 0) * scale
        send_ref[...] = ms[pl.ds(pl.multiple_of((1 - info_ref[1]) * half, half), half), :]
        mine_ref[...] = ms[pl.ds(pl.multiple_of(info_ref[1] * half, half), half), :]

    full = lambda a: pl.BlockSpec(a.shape, lambda j, *_: (0, 0), pipeline_mode=pl.Buffered(1))
    col = lambda h: pl.BlockSpec((h, tile), lambda j, *_: (0, j))
    out = jax.ShapeDtypeStruct((half, cols), F32)
    return pl.pallas_call(
        kernel,
        out_shape=(out, out, jax.ShapeDtypeStruct((rows, width), F32)),
        grid_spec=pltpu.PrefetchScalarGridSpec(
            num_scalar_prefetch=1,
            grid=(cols // tile,),
            in_specs=[
                col(rows),
                pl.BlockSpec(
                    (rows, width), lambda j, *_: (0, base // width), pipeline_mode=pl.Buffered(1)
                ),
            ]
            + [full(p) for p in parts],
            out_specs=(col(half), col(half), pl.BlockSpec((rows, width), lambda j, *_: (0, 0))),
            scratch_shapes=[
                pltpu.VMEM((width, 3 * rows), BF16),
                pltpu.VMEM((3 * rows, tile), BF16),
                pltpu.VMEM((width, tile), F32),
            ],
        ),
        compiler_params=pltpu.CompilerParams(vmem_limit_bytes=58 << 20),
        cost_estimate=pl.CostEstimate(
            flops=6 * rows * cols * width, bytes_accessed=4 * rows * cols, transcendentals=0
        ),
        name="panel_dot",
    )(info, snapshots, snapshots, *parts)


def part_size(rows, parts):
    return -(-rows // (8 * parts)) * 8


def merge(arrays):
    def kernel(*refs):
        total = refs[0][...]
        for ref in refs[1:-1]:
            total = total + ref[...]
        refs[-1][...] = total

    return pl.pallas_call(
        kernel,
        out_shape=jax.ShapeDtypeStruct(arrays[0].shape, F32),
        in_specs=[VMEM] * len(arrays),
        out_specs=VMEM,
        cost_estimate=pl.CostEstimate(flops=MERGE_COST, bytes_accessed=1 << 20, transcendentals=0),
        name="merge",
    )(*arrays)


def spread_out(x, n):
    rows, parts = x.shape[0], n - 1
    size = part_size(rows, parts)
    got = []
    for k in reversed(range(parts)):
        start = min(k * size, rows - size)
        got.append(lax.ppermute(x[start : start + size], "cols", [(0, k + 1)]))
    return merge(got)


def spread_round(mine, n):
    got, parts = [mine], n - 1
    for k in range(1, parts):
        pairs = [(1 + i, 1 + (i + k) % parts) for i in range(parts)]
        got.append(lax.ppermute(mine, "cols", pairs))
    return got


def after(x, *others):
    return lax.optimization_barrier((x, others))[0]


def swap(n, k):
    return [(i, i ^ k) for i in range(n)]


def take(a, start, size):
    return lax.dynamic_slice_in_dim(a, start, size, 0)


def join_cores(send, mine, n):
    return mine + lax.ppermute(send, "rows", swap(n, 1))


def scatter_chips(mine, n):
    chips = n // 2
    chip = lax.axis_index("rows") >> 1
    piece = mine.shape[0] // chips
    own = take(mine, chip * piece, piece)
    for k in range(1, chips):
        own = own + lax.ppermute(take(mine, (chip ^ k) * piece, piece), "rows", swap(n, 2 * k))
    return own


def gather_rows(own, n):
    got = [own] + [lax.ppermute(own, "rows", swap(n, 2 * k)) for k in range(1, n // 2)]
    other = [lax.ppermute(g, "rows", swap(n, 1)) for g in got]
    return got + other, [(0, k) for k in range(n // 2)] + [(1, k) for k in range(n // 2)]


def shards(snapshots):
    rows_dev, cols_dev = snapshots.shape
    n_rows, n_cols = lax.axis_size("rows"), lax.axis_size("cols")
    total_rows = rows_dev * n_rows
    z, index = lax.axis_index("cols"), lax.axis_index("rows")
    core = index & 1
    parts = n_cols - 1
    size = part_size(rows_dev, parts)
    starts = [jnp.minimum(((z - 1 - k) % parts) * size, rows_dev - size) for k in range(parts)]
    info = jnp.stack([z, core, index >> 1] + starts).astype(jnp.int32)
    half = PB // 2
    panel = snapshots[:, :PB]
    dot = lambda got, base: panel_dot(
        info, snapshots, got, size, base, half, 1.0 / total_rows
    )

    mine_a = spread_out(panel[:, :half], n_cols)
    gram = mm(panel, panel, 0, 0, HIGHEST) / total_rows
    joined = join_cores(take(gram, (1 - core) * half, half), take(gram, core * half, half), n_rows)
    share = scatter_chips(joined, n_rows)
    far = [lax.ppermute(share, "cols", [(0, k)]) for k in reversed(range(1, n_cols))]
    got_a = spread_round(mine_a, n_cols)
    mine_b = spread_out(after(panel[:, half:], mine_a), n_cols)
    share = jnp.where(z == 0, share, sum(far, jnp.zeros_like(share)))
    grams, places = gather_rows(share, n_rows)

    send, keep, panel_a = dot(after(got_a, far), 0)
    state = chol_part(info, 0, 1, pieces=after(grams, send, mine_b), places=places)
    joined = join_cores(send, keep, n_rows)
    own_a = scatter_chips(joined, n_rows)
    got_b = spread_round(mine_b, n_cols)
    state = chol_part(info, 1, 2, state=after(state, joined))
    pieces_a, where = gather_rows(own_a, n_rows)
    send, keep, panel_b = dot(after(got_b, own_a, state), half)
    joined = join_cores(send, keep, n_rows)
    own_b = scatter_chips(joined, n_rows)
    state = chol_part(info, 2, 3, state=after(state, joined))
    pieces_b, _ = gather_rows(own_b, n_rows)
    _, factor, linv = chol_part(info, 3, 4, state=after(state, own_b))
    layout = [(base,) + w for base in (0, half) for w in where]
    return finish(
        info, snapshots, [panel_a, panel_b], linv, factor, pieces_a + pieces_b, layout
    )


def solution(mesh):
    in_specs = (P("rows", "cols"),)
    out_specs = (P("rows", "cols"), P(None, "cols"))
    return jax.shard_map(shards, mesh=mesh, in_specs=in_specs, out_specs=out_specs, check_vma=False)
```

```python
import jax
import jax.numpy as jnp
from jax import lax
from jax.experimental import pallas as pl
from jax.experimental.pallas import tpu as pltpu
from jax.sharding import PartitionSpec as P

PB = 512
NB = 128
F32 = jnp.float32
BF16 = jnp.bfloat16
HIGHEST = lax.Precision.HIGHEST
VMEM = pl.BlockSpec(memory_space=pltpu.VMEM)


def mm(a, b, da, db, precision=None):
    return lax.dot_general(
        a, b, (((da,), (db,)), ((), ())), precision=precision, preferred_element_type=F32
    )


def split(x):
    high = x.astype(BF16)
    return high, (x - high.astype(F32)).astype(BF16)


def diag_block(d_ref, z_ref, f_ref):
    a_all = d_ref[...]
    row = lax.broadcasted_iota(jnp.int32, (NB, NB), 0)
    col = lax.broadcasted_iota(jnp.int32, (NB, NB), 1)
    z_all = jnp.where(row == col, 1.0, 0.0).astype(F32)
    lane = lax.broadcasted_iota(jnp.int32, (1, NB), 1)
    for j in range(0, NB, 4):
        base = (j // 8) * 8
        if a_all.shape[0] != NB - base:
            a_all, z_all = a_all[8:], z_all[8:]
        i, n = j - base, NB - base
        t = [a_all[i + k : i + k + 1, :] for k in range(4)]
        u = [z_all[i + k : i + k + 1, :] for k in range(4)]
        c = [jnp.broadcast_to(a_all[:, j + k : j + k + 1], (n, NB)) for k in range(4)]
        e = {
            (k, m): jnp.broadcast_to(t[k][:, j + m : j + m + 1], (1, NB))
            for k in range(4)
            for m in range(k, 4)
        }
        inv, low = [], {}
        for k in range(4):
            inv.append(1.0 / e[k, k])
            for m in range(k + 1, 4):
                low[m, k] = e[k, m] * inv[k]
            for m in range(k + 1, 4):
                for q in range(m, 4):
                    e[m, q] = e[m, q] - low[m, k] * e[k, q]
        for k in range(4):
            for m in range(k):
                t[k] = t[k] - low[k, m] * t[m]
                u[k] = u[k] - low[k, m] * u[m]
        x, y = [None] * 4, [None] * 4
        for k in reversed(range(4)):
            x[k], y[k] = t[k] * inv[k], u[k] * inv[k]
            for m in range(k + 1, 4):
                x[k] = x[k] - low[m, k] * x[m]
                y[k] = y[k] - low[m, k] * y[m]
        for k in range(4):
            root = lax.rsqrt(e[k, k])
            f_ref[j + k : j + k + 1, :] = jnp.where(lane >= j + k, t[k] * root, 0.0)
            z_ref[j + k : j + k + 1, :] = u[k] * root
        if j + 4 < NB:
            a_all = a_all - ((c[0] * x[0] + c[1] * x[1]) + (c[2] * x[2] + c[3] * x[3]))
            z_all = z_all - ((c[0] * y[0] + c[1] * y[1]) + (c[2] * y[2] + c[3] * y[3]))


def chol_part(info, first, last, pieces=None, places=None, state=None):
    fresh = pieces is not None
    arrays = pieces if fresh else state
    n = arrays[0].shape[1]
    nb = n // NB
    n_in = len(arrays)

    def kernel(info_ref, *refs):
        work, f_out, l_out = refs[n_in : n_in + 3]
        diag, zs, fs = refs[n_in + 3 :]
        if fresh:
            chips = n_in // 2
            for ref, (core, chip) in zip(refs, places):
                h = ref.shape[0]
                off = (info_ref[1] ^ core) * (h * chips) + (info_ref[2] ^ chip) * h
                work[pl.ds(pl.multiple_of(off, 8), h), :] = ref[...]
            f_out[...] = jnp.zeros_like(f_out)
            l_out[...] = jnp.zeros_like(l_out)

        def body(k, carry):
            o = pl.multiple_of(k * NB, NB)
            diag[...] = work[pl.ds(o, NB), pl.ds(o, NB)]
            diag_block(diag, zs, fs)
            for kk in range(first, last):

                @pl.when(k == kk)
                def _():
                    o, e = kk * NB, kk * NB + NB
                    z = zs[...]
                    f_out[o:e, o:e] = fs[...]
                    lk = z
                    if kk > 0:
                        lk = jnp.concatenate([mm(z, l_out[o:e, :o], 1, 0, HIGHEST), z], axis=1)
                    l_out[o:e, :e] = lk
                    if kk < nb - 1:
                        u = mm(z, work[o:e, e:], 1, 0, HIGHEST)
                        f_out[o:e, e:] = u
                        work[e:, e:] -= mm(u, u, 0, 0, HIGHEST)
                        l_out[e:, :e] -= mm(u, lk, 0, 0, HIGHEST)

            return carry

        lax.fori_loop(first, last, body, 0)

    shape = jax.ShapeDtypeStruct((n, n), F32)
    return pl.pallas_call(
        kernel,
        out_shape=(shape, shape, shape),
        in_specs=[pl.BlockSpec(memory_space=pltpu.SMEM)] + [VMEM] * n_in,
        out_specs=(VMEM, VMEM, VMEM),
        scratch_shapes=[pltpu.VMEM((NB, NB), F32)] * 3,
        input_output_aliases={} if fresh else {1: 0, 2: 1, 3: 2},
        compiler_params=pltpu.CompilerParams(vmem_limit_bytes=16 << 20),
        cost_estimate=pl.CostEstimate(
            flops=(last - first) * 8 * 10**9, bytes_accessed=3 << 20, transcendentals=0
        ),
        name="chol_part",
    )(info, *arrays)


def finish(info, snapshots, panels, linv, factor, pieces, layout, tile=512):
    rows, cols = snapshots.shape
    n_pieces, n_panels = len(pieces), len(panels)
    chips = 1 + max(chip for _, _, chip in layout)
    bases = [sum(p.shape[1] for p in panels[:i]) for i in range(n_panels)]

    def kernel(info_ref, s_ref, l_ref, f_ref, *rest):
        p_refs, rest = rest[:n_panels], rest[n_panels:]
        m_refs = rest[:n_pieces]
        up_ref, co_ref, bs, b3, l3, ms, m3, p3 = rest[n_pieces:]
        j = pl.program_id(0)

        @pl.when(j == 0)
        def _():
            lh, ll = split(l_ref[...])
            l3[:, :PB], l3[:, PB : 2 * PB], l3[:, 2 * PB :] = lh, lh, ll
            for r in range(0, rows, 256):
                b = 0.0
                for base, p_ref in zip(bases, p_refs):
                    end = base + p_ref.shape[1]
                    ph, plow = split(p_ref[r : r + 256, :])
                    lhs = jnp.concatenate([ph, ph, plow], axis=1)
                    rhs = jnp.concatenate([lh[:, base:end], ll[:, base:end], lh[:, base:end]], axis=1)
                    b = b + mm(lhs, rhs, 1, 1)
                bs[r : r + 256, :] = b
                bh, bl = split(b)
                b3[r : r + 256, :PB], b3[r : r + 256, PB : 2 * PB] = bh, bh
                b3[r : r + 256, 2 * PB :] = bl

        for ref, (base, core, chip) in zip(m_refs, layout):
            h = ref.shape[0]
            off = base + (info_ref[1] ^ core) * (h * chips) + (info_ref[2] ^ chip) * h
            ms[pl.ds(pl.multiple_of(off, 8), h), :] = ref[...]
        mh, ml = split(ms[...])
        m3[:PB, :], m3[PB : 2 * PB, :], m3[2 * PB :, :] = mh, ml, mh
        proj = mm(l3[...], m3[...], 1, 0)
        ph, plow = split(proj)
        p3[:PB, :], p3[PB : 2 * PB, :], p3[2 * PB :, :] = ph, plow, ph
        co_ref[...] = proj
        up_ref[...] = s_ref[...] - mm(b3[...], p3[...], 1, 0)
        for t in range(PB // tile):

            @pl.when((info_ref[0] == 0) & (j == t))
            def _():
                co_ref[...] = f_ref[:, t * tile : (t + 1) * tile]
                up_ref[...] = bs[:, t * tile : (t + 1) * tile]

    col = lambda h: pl.BlockSpec((h, tile), lambda j, *_: (0, j))
    return pl.pallas_call(
        kernel,
        out_shape=(
            jax.ShapeDtypeStruct((rows, cols), F32),
            jax.ShapeDtypeStruct((PB, cols), F32),
        ),
        grid_spec=pltpu.PrefetchScalarGridSpec(
            num_scalar_prefetch=1,
            grid=(cols // tile,),
            in_specs=[col(rows), VMEM, VMEM]
            + [VMEM for _ in panels]
            + [col(p.shape[0]) for p in pieces],
            out_specs=(col(rows), col(PB)),
            scratch_shapes=[
                pltpu.VMEM((rows, PB), F32),
                pltpu.VMEM((rows, 3 * PB), BF16),
                pltpu.VMEM((PB, 3 * PB), BF16),
                pltpu.VMEM((PB, tile), F32),
                pltpu.VMEM((3 * PB, tile), BF16),
                pltpu.VMEM((3 * PB, tile), BF16),
            ],
        ),
        compiler_params=pltpu.CompilerParams(vmem_limit_bytes=58 << 20),
        cost_estimate=pl.CostEstimate(
            flops=6 * PB * cols * (rows + PB), bytes_accessed=8 * rows * cols, transcendentals=0
        ),
        name="finish",
    )(info, snapshots, linv, factor, *panels, *pieces)


def panel_dot(info, snapshots, parts, size, base, width, scale, tile=512):
    rows, cols = snapshots.shape
    half = width // 2
    n_parts = len(parts)

    def kernel(info_ref, s_ref, own_ref, *rest):
        part_refs = rest[:n_parts]
        send_ref, mine_ref, p_ref, pt3, s3, ms = rest[n_parts:]
        j = pl.program_id(0)

        @pl.when((j == 0) & (info_ref[0] == 0))
        def _():
            p_ref[...] = own_ref[...]

        if n_parts:

            @pl.when((j == 0) & (info_ref[0] != 0))
            def _():
                for k, ref in enumerate(part_refs):
                    start = pl.multiple_of(info_ref[3 + k], 8)
                    p_ref[pl.ds(start, size), :] = ref[...]

        @pl.when(j == 0)
        def _():
            for r in range(0, rows, 256):
                ph, plow = split(p_ref[r : r + 256, :])
                pt = ph.T
                pt3[:, r : r + 256], pt3[:, rows + r : rows + r + 256] = pt, pt
                pt3[:, 2 * rows + r : 2 * rows + r + 256] = plow.T

        sh, sl = split(s_ref[...])
        s3[:rows, :], s3[rows : 2 * rows, :], s3[2 * rows :, :] = sh, sl, sh
        ms[...] = mm(pt3[...], s3[...], 1, 0) * scale
        send_ref[...] = ms[pl.ds(pl.multiple_of((1 - info_ref[1]) * half, half), half), :]
        mine_ref[...] = ms[pl.ds(pl.multiple_of(info_ref[1] * half, half), half), :]

    full = lambda a: pl.BlockSpec(a.shape, lambda j, *_: (0, 0), pipeline_mode=pl.Buffered(1))
    col = lambda h: pl.BlockSpec((h, tile), lambda j, *_: (0, j))
    out = jax.ShapeDtypeStruct((half, cols), F32)
    return pl.pallas_call(
        kernel,
        out_shape=(out, out, jax.ShapeDtypeStruct((rows, width), F32)),
        grid_spec=pltpu.PrefetchScalarGridSpec(
            num_scalar_prefetch=1,
            grid=(cols // tile,),
            in_specs=[
                col(rows),
                pl.BlockSpec(
                    (rows, width), lambda j, *_: (0, base // width), pipeline_mode=pl.Buffered(1)
                ),
            ]
            + [full(p) for p in parts],
            out_specs=(col(half), col(half), pl.BlockSpec((rows, width), lambda j, *_: (0, 0))),
            scratch_shapes=[
                pltpu.VMEM((width, 3 * rows), BF16),
                pltpu.VMEM((3 * rows, tile), BF16),
                pltpu.VMEM((width, tile), F32),
            ],
        ),
        compiler_params=pltpu.CompilerParams(vmem_limit_bytes=58 << 20),
        cost_estimate=pl.CostEstimate(
            flops=6 * rows * cols * width, bytes_accessed=4 * rows * cols, transcendentals=0
        ),
        name="panel_dot",
    )(info, snapshots, snapshots, *parts)


def part_size(rows, parts):
    return -(-rows // (8 * parts)) * 8


def spread_out(x, n):
    rows, parts = x.shape[0], n - 1
    size = part_size(rows, parts)
    got = []
    for k in reversed(range(parts)):
        start = min(k * size, rows - size)
        got.append(lax.ppermute(x[start : start + size], "cols", [(0, k + 1)]))
    return sum(got[1:], got[0])


def spread_round(mine, n):
    got, parts = [mine], n - 1
    for k in range(1, parts):
        pairs = [(1 + i, 1 + (i + k) % parts) for i in range(parts)]
        got.append(lax.ppermute(mine, "cols", pairs))
    return got


def after(x, *others):
    return lax.optimization_barrier((x, others))[0]


def swap(n, k):
    return [(i, i ^ k) for i in range(n)]


def take(a, start, size):
    return lax.dynamic_slice_in_dim(a, start, size, 0)


def join_cores(send, mine, n):
    return mine + lax.ppermute(send, "rows", swap(n, 1))


def scatter_chips(mine, n):
    chips = n // 2
    chip = lax.axis_index("rows") >> 1
    piece = mine.shape[0] // chips
    own = take(mine, chip * piece, piece)
    for k in range(1, chips):
        own = own + lax.ppermute(take(mine, (chip ^ k) * piece, piece), "rows", swap(n, 2 * k))
    return own


def gather_rows(own, n):
    got = [own] + [lax.ppermute(own, "rows", swap(n, 2 * k)) for k in range(1, n // 2)]
    other = [lax.ppermute(g, "rows", swap(n, 1)) for g in got]
    return got + other, [(0, k) for k in range(n // 2)] + [(1, k) for k in range(n // 2)]


def shards(snapshots):
    rows_dev, cols_dev = snapshots.shape
    n_rows, n_cols = lax.axis_size("rows"), lax.axis_size("cols")
    total_rows = rows_dev * n_rows
    z, index = lax.axis_index("cols"), lax.axis_index("rows")
    core = index & 1
    parts = n_cols - 1
    size = part_size(rows_dev, parts)
    starts = [jnp.minimum(((z - 1 - k) % parts) * size, rows_dev - size) for k in range(parts)]
    info = jnp.stack([z, core, index >> 1] + starts).astype(jnp.int32)
    half = PB // 2
    panel = snapshots[:, :PB]
    dot = lambda got, base: panel_dot(
        info, snapshots, got, size, base, half, 1.0 / total_rows
    )

    mine_a = spread_out(panel[:, :half], n_cols)
    gram = mm(panel, panel, 0, 0, HIGHEST) / total_rows
    joined = join_cores(take(gram, (1 - core) * half, half), take(gram, core * half, half), n_rows)
    share = scatter_chips(joined, n_rows)
    far = [lax.ppermute(share, "cols", [(0, k)]) for k in reversed(range(1, n_cols))]
    got_a = spread_round(mine_a, n_cols)
    mine_b = spread_out(after(panel[:, half:], mine_a), n_cols)
    share = jnp.where(z == 0, share, sum(far, jnp.zeros_like(share)))
    grams, places = gather_rows(share, n_rows)

    send, keep, panel_a = dot(after(got_a, far, mine_b), 0)
    state = chol_part(info, 0, 1, pieces=after(grams, send, mine_b), places=places)
    joined = join_cores(send, keep, n_rows)
    own_a = scatter_chips(joined, n_rows)
    got_b = spread_round(mine_b, n_cols)
    state = chol_part(info, 1, 2, state=after(state, own_a))
    pieces_a, where = gather_rows(own_a, n_rows)
    send, keep, panel_b = dot(after(got_b, pieces_a, state), half)
    joined = join_cores(send, keep, n_rows)
    own_b = scatter_chips(joined, n_rows)
    state = chol_part(info, 2, 3, state=after(state, joined))
    pieces_b, _ = gather_rows(own_b, n_rows)
    _, factor, linv = chol_part(info, 3, 4, state=after(state, own_b))
    layout = [(base,) + w for base in (0, half) for w in where]
    return finish(
        info, snapshots, [panel_a, panel_b], linv, factor, pieces_a + pieces_b, layout
    )


def solution(mesh):
    in_specs = (P("rows", "cols"),)
    out_specs = (P("rows", "cols"), P(None, "cols"))
    return jax.shard_map(shards, mesh=mesh, in_specs=in_specs, out_specs=out_specs, check_vma=False)
```

```python
import jax
import jax.numpy as jnp
from jax import lax
from jax.experimental import pallas as pl
from jax.experimental.pallas import tpu as pltpu
from jax.sharding import PartitionSpec as P

PB = 512
NB = 128
F32 = jnp.float32
BF16 = jnp.bfloat16
HIGHEST = lax.Precision.HIGHEST
VMEM = pl.BlockSpec(memory_space=pltpu.VMEM)


def cost(flops):
    return pl.CostEstimate(flops=flops, bytes_accessed=1 << 20, transcendentals=0)


def mm(a, b, da, db, precision=None):
    return lax.dot_general(
        a, b, (((da,), (db,)), ((), ())), precision=precision, preferred_element_type=F32
    )


def split(x):
    high = x.astype(BF16)
    return high, (x - high.astype(F32)).astype(BF16)


def diag_block(d_ref, z_ref, f_ref):
    a_all = d_ref[...]
    row = lax.broadcasted_iota(jnp.int32, (NB, NB), 0)
    col = lax.broadcasted_iota(jnp.int32, (NB, NB), 1)
    z_all = jnp.where(row == col, 1.0, 0.0).astype(F32)
    lane = lax.broadcasted_iota(jnp.int32, (1, NB), 1)
    for j in range(0, NB, 4):
        base = (j // 8) * 8
        if a_all.shape[0] != NB - base:
            a_all, z_all = a_all[8:], z_all[8:]
        i, n = j - base, NB - base
        t = [a_all[i + k : i + k + 1, :] for k in range(4)]
        u = [z_all[i + k : i + k + 1, :] for k in range(4)]
        c = [jnp.broadcast_to(a_all[:, j + k : j + k + 1], (n, NB)) for k in range(4)]
        e = {
            (k, m): jnp.broadcast_to(t[k][:, j + m : j + m + 1], (1, NB))
            for k in range(4)
            for m in range(k, 4)
        }
        inv, low = [], {}
        for k in range(4):
            inv.append(1.0 / e[k, k])
            for m in range(k + 1, 4):
                low[m, k] = e[k, m] * inv[k]
            for m in range(k + 1, 4):
                for q in range(m, 4):
                    e[m, q] = e[m, q] - low[m, k] * e[k, q]
        for k in range(4):
            for m in range(k):
                t[k] = t[k] - low[k, m] * t[m]
                u[k] = u[k] - low[k, m] * u[m]
        x, y = [None] * 4, [None] * 4
        for k in reversed(range(4)):
            x[k], y[k] = t[k] * inv[k], u[k] * inv[k]
            for m in range(k + 1, 4):
                x[k] = x[k] - low[m, k] * x[m]
                y[k] = y[k] - low[m, k] * y[m]
        for k in range(4):
            root = lax.rsqrt(e[k, k])
            f_ref[j + k : j + k + 1, :] = jnp.where(lane >= j + k, t[k] * root, 0.0)
            z_ref[j + k : j + k + 1, :] = u[k] * root
        if j + 4 < NB:
            a_all = a_all - ((c[0] * x[0] + c[1] * x[1]) + (c[2] * x[2] + c[3] * x[3]))
            z_all = z_all - ((c[0] * y[0] + c[1] * y[1]) + (c[2] * y[2] + c[3] * y[3]))


def chol_part(info, first, last, pieces=None, places=None, state=None):
    fresh = pieces is not None
    arrays = pieces if fresh else state
    n = arrays[0].shape[1]
    nb = n // NB
    n_in = len(arrays)

    def kernel(info_ref, *refs):
        work, f_out, l_out = refs[n_in : n_in + 3]
        diag, zs, fs = refs[n_in + 3 :]
        if fresh:
            chips = n_in // 2
            for ref, (core, chip) in zip(refs, places):
                h = ref.shape[0]
                off = (info_ref[1] ^ core) * (h * chips) + (info_ref[2] ^ chip) * h
                work[pl.ds(pl.multiple_of(off, 8), h), :] = ref[...]
            f_out[...] = jnp.zeros_like(f_out)
            l_out[...] = jnp.zeros_like(l_out)

        def body(k, carry):
            o = pl.multiple_of(k * NB, NB)
            diag[...] = work[pl.ds(o, NB), pl.ds(o, NB)]
            diag_block(diag, zs, fs)
            for kk in range(first, last):

                @pl.when(k == kk)
                def _():
                    o, e = kk * NB, kk * NB + NB
                    z = zs[...]
                    f_out[o:e, o:e] = fs[...]
                    lk = z
                    if kk > 0:
                        lk = jnp.concatenate([mm(z, l_out[o:e, :o], 1, 0, HIGHEST), z], axis=1)
                    l_out[o:e, :e] = lk
                    if kk < nb - 1:
                        u = mm(z, work[o:e, e:], 1, 0, HIGHEST)
                        f_out[o:e, e:] = u
                        work[e:, e:] -= mm(u, u, 0, 0, HIGHEST)
                        l_out[e:, :e] -= mm(u, lk, 0, 0, HIGHEST)

            return carry

        lax.fori_loop(first, last, body, 0)

    shape = jax.ShapeDtypeStruct((n, n), F32)
    return pl.pallas_call(
        kernel,
        out_shape=(shape, shape, shape),
        in_specs=[pl.BlockSpec(memory_space=pltpu.SMEM)] + [VMEM] * n_in,
        out_specs=(VMEM, VMEM, VMEM),
        scratch_shapes=[pltpu.VMEM((NB, NB), F32)] * 3,
        input_output_aliases={} if fresh else {1: 0, 2: 1, 3: 2},
        compiler_params=pltpu.CompilerParams(vmem_limit_bytes=16 << 20),
        cost_estimate=cost((last - first) * 8 * 10**9),
        name="chol_part",
    )(info, *arrays)


def finish(info, rest, panels, linv, factor, pieces, layout, half, coeffs=None, tile=512):
    rows, cols = rest.shape
    n_pieces, n_panels = len(pieces), len(panels)
    chips = 1 + max(chip for _, _, chip in layout)
    width = PB // 2
    depth = width * n_panels
    top = half * width

    def kernel(info_ref, s_ref, l_ref, f_ref, *refs):
        p_refs, refs = refs[:n_panels], refs[n_panels:]
        m_refs, refs = refs[:n_pieces], refs[n_pieces:]
        up_ref, co_ref, bs, b3, l3, ms, m3, p3 = refs[-8:]
        j = pl.program_id(0)

        @pl.when(j == 0)
        def _():
            lh, ll = split(l_ref[top : top + width, :depth])
            l3[:, :depth], l3[:, depth : 2 * depth], l3[:, 2 * depth :] = lh, lh, ll
            for r in range(0, rows, 256):
                b = 0.0
                for k, p_ref in enumerate(p_refs):
                    ph, plow = split(p_ref[r : r + 256, :])
                    kh, kl = lh[:, k * width : (k + 1) * width], ll[:, k * width : (k + 1) * width]
                    lhs = jnp.concatenate([ph, ph, plow], axis=1)
                    b = b + mm(lhs, jnp.concatenate([kh, kl, kh], axis=1), 1, 1)
                bs[r : r + 256, :] = b
                bh, bl = split(b)
                b3[r : r + 256, :width], b3[r : r + 256, width : 2 * width] = bh, bh
                b3[r : r + 256, 2 * width :] = bl

        for ref, (base, core, chip) in zip(m_refs, layout):
            h = ref.shape[0]
            off = base + (info_ref[1] ^ core) * (h * chips) + (info_ref[2] ^ chip) * h
            ms[pl.ds(pl.multiple_of(off, 8), h), :] = ref[...]
        mh, ml = split(ms[...])
        m3[:depth, :], m3[depth : 2 * depth, :], m3[2 * depth :, :] = mh, ml, mh
        proj = mm(l3[...], m3[...], 1, 0)
        ph, plow = split(proj)
        p3[:width, :], p3[width : 2 * width, :], p3[2 * width :, :] = ph, plow, ph
        co_ref[...] = proj
        up_ref[...] = s_ref[...] - mm(b3[...], p3[...], 1, 0)

        @pl.when((info_ref[0] == 0) & (j == 0))
        def _():
            co_ref[...] = f_ref[top : top + width, :]
            if half:
                up_ref[:, :top] = s_ref[:, :top]
            up_ref[:, top : top + width] = bs[...]

    col = lambda h: pl.BlockSpec((h, tile), lambda j, *_: (0, j))
    operands = [rest, linv, factor, *panels, *pieces]
    specs = [col(rows), VMEM, VMEM] + [VMEM] * n_panels + [col(p.shape[0]) for p in pieces]
    aliases = {}
    if half:
        operands.append(coeffs)
        specs.append(pl.BlockSpec(memory_space=pl.ANY))
        aliases = {1: 0, len(operands): 1}
    return pl.pallas_call(
        kernel,
        out_shape=(
            jax.ShapeDtypeStruct((rows, cols), F32),
            jax.ShapeDtypeStruct((PB, cols), F32),
        ),
        grid_spec=pltpu.PrefetchScalarGridSpec(
            num_scalar_prefetch=1,
            grid=(cols // tile,),
            in_specs=specs,
            out_specs=(col(rows), pl.BlockSpec((width, tile), lambda j, *_: (half, j))),
            scratch_shapes=[
                pltpu.VMEM((rows, width), F32),
                pltpu.VMEM((rows, 3 * width), BF16),
                pltpu.VMEM((width, 3 * depth), BF16),
                pltpu.VMEM((depth, tile), F32),
                pltpu.VMEM((3 * depth, tile), BF16),
                pltpu.VMEM((3 * width, tile), BF16),
            ],
        ),
        input_output_aliases=aliases,
        compiler_params=pltpu.CompilerParams(vmem_limit_bytes=56 << 20),
        cost_estimate=cost(10**10),
        name="finish",
    )(info, *operands)


def panel_dot(info, snapshots, parts, size, base, width, scale, tile=512):
    rows, cols = snapshots.shape
    half = width // 2
    n_parts = len(parts)

    def kernel(info_ref, s_ref, own_ref, *rest):
        part_refs = rest[:n_parts]
        send_ref, mine_ref, p_ref, pt3, s3, ms = rest[n_parts:]
        j = pl.program_id(0)

        @pl.when((j == 0) & (info_ref[0] == 0))
        def _():
            p_ref[...] = own_ref[...]

        if n_parts:

            @pl.when((j == 0) & (info_ref[0] != 0))
            def _():
                for k, ref in enumerate(part_refs):
                    start = pl.multiple_of(info_ref[3 + k], 8)
                    p_ref[pl.ds(start, size), :] = ref[...]

        @pl.when(j == 0)
        def _():
            for r in range(0, rows, 256):
                ph, plow = split(p_ref[r : r + 256, :])
                pt = ph.T
                pt3[:, r : r + 256], pt3[:, rows + r : rows + r + 256] = pt, pt
                pt3[:, 2 * rows + r : 2 * rows + r + 256] = plow.T

        sh, sl = split(s_ref[...])
        s3[:rows, :], s3[rows : 2 * rows, :], s3[2 * rows :, :] = sh, sl, sh
        ms[...] = mm(pt3[...], s3[...], 1, 0) * scale
        send_ref[...] = ms[pl.ds(pl.multiple_of((1 - info_ref[1]) * half, half), half), :]
        mine_ref[...] = ms[pl.ds(pl.multiple_of(info_ref[1] * half, half), half), :]

    full = lambda a: pl.BlockSpec(a.shape, lambda j, *_: (0, 0), pipeline_mode=pl.Buffered(1))
    col = lambda h: pl.BlockSpec((h, tile), lambda j, *_: (0, j))
    out = jax.ShapeDtypeStruct((half, cols), F32)
    return pl.pallas_call(
        kernel,
        out_shape=(out, out, jax.ShapeDtypeStruct((rows, width), F32)),
        grid_spec=pltpu.PrefetchScalarGridSpec(
            num_scalar_prefetch=1,
            grid=(cols // tile,),
            in_specs=[
                col(rows),
                pl.BlockSpec(
                    (rows, width), lambda j, *_: (0, base // width), pipeline_mode=pl.Buffered(1)
                ),
            ]
            + [full(p) for p in parts],
            out_specs=(col(half), col(half), pl.BlockSpec((rows, width), lambda j, *_: (0, 0))),
            scratch_shapes=[
                pltpu.VMEM((width, 3 * rows), BF16),
                pltpu.VMEM((3 * rows, tile), BF16),
                pltpu.VMEM((width, tile), F32),
            ],
        ),
        compiler_params=pltpu.CompilerParams(vmem_limit_bytes=58 << 20),
        cost_estimate=cost(6 * rows * cols * width),
        name="panel_dot",
    )(info, snapshots, snapshots, *parts)


def part_size(rows, parts):
    return -(-rows // (8 * parts)) * 8


def spread_out(x, n):
    rows, parts = x.shape[0], n - 1
    size = part_size(rows, parts)
    got = []
    for k in reversed(range(parts)):
        start = min(k * size, rows - size)
        got.append(lax.ppermute(x[start : start + size], "cols", [(0, k + 1)]))
    return sum(got[1:], got[0])


def spread_round(mine, n):
    got, parts = [mine], n - 1
    for k in range(1, parts):
        pairs = [(1 + i, 1 + (i + k) % parts) for i in range(parts)]
        got.append(lax.ppermute(mine, "cols", pairs))
    return got


def after(x, *others):
    return lax.optimization_barrier((x, others))[0]


def swap(n, k):
    return [(i, i ^ k) for i in range(n)]


def take(a, start, size):
    return lax.dynamic_slice_in_dim(a, start, size, 0)


def join_cores(send, mine, n):
    return mine + lax.ppermute(send, "rows", swap(n, 1))


def scatter_chips(mine, n):
    chips = n // 2
    chip = lax.axis_index("rows") >> 1
    piece = mine.shape[0] // chips
    own = take(mine, chip * piece, piece)
    for k in range(1, chips):
        own = own + lax.ppermute(take(mine, (chip ^ k) * piece, piece), "rows", swap(n, 2 * k))
    return own


def gather_rows(own, n):
    got = [own] + [lax.ppermute(own, "rows", swap(n, 2 * k)) for k in range(1, n // 2)]
    other = [lax.ppermute(g, "rows", swap(n, 1)) for g in got]
    return got + other, [(0, k) for k in range(n // 2)] + [(1, k) for k in range(n // 2)]


def shards(snapshots):
    rows_dev, cols_dev = snapshots.shape
    n_rows, n_cols = lax.axis_size("rows"), lax.axis_size("cols")
    total_rows = rows_dev * n_rows
    z, index = lax.axis_index("cols"), lax.axis_index("rows")
    core = index & 1
    parts = n_cols - 1
    size = part_size(rows_dev, parts)
    starts = [jnp.minimum(((z - 1 - k) % parts) * size, rows_dev - size) for k in range(parts)]
    info = jnp.stack([z, core, index >> 1] + starts).astype(jnp.int32)
    half = PB // 2
    panel = snapshots[:, :PB]
    dot = lambda got, base: panel_dot(
        info, snapshots, got, size, base, half, 1.0 / total_rows
    )

    mine_a = spread_out(panel[:, :half], n_cols)
    gram = mm(panel, panel, 0, 0, HIGHEST) / total_rows
    joined = join_cores(take(gram, (1 - core) * half, half), take(gram, core * half, half), n_rows)
    share = scatter_chips(joined, n_rows)
    far = [lax.ppermute(share, "cols", [(0, k)]) for k in reversed(range(1, n_cols))]
    got_a = spread_round(mine_a, n_cols)
    mine_b = spread_out(after(panel[:, half:], mine_a), n_cols)
    share = jnp.where(z == 0, share, sum(far, jnp.zeros_like(share)))
    grams, places = gather_rows(share, n_rows)

    send, keep, panel_a = dot(after(got_a, far, mine_b), 0)
    joined = join_cores(send, keep, n_rows)
    got_b = spread_round(mine_b, n_cols)
    own_a = scatter_chips(joined, n_rows)
    state = chol_part(info, 0, 2, pieces=after(grams, joined, mine_b), places=places)
    pieces_a, where = gather_rows(own_a, n_rows)
    send, keep, panel_b = dot(after(got_b, own_a, state), half)
    joined = join_cores(send, keep, n_rows)
    own_b = scatter_chips(joined, n_rows)
    state = chol_part(info, 2, 3, state=after(state, joined))
    _, factor, linv = chol_part(info, 3, 4, state=after(state, own_b))
    pieces_b, _ = gather_rows(own_b, n_rows)
    layout = [(base,) + w for base in (0, half) for w in where]
    rest, coeffs = finish(
        info, snapshots, [panel_a], linv, factor, pieces_a, layout[: len(where)], 0
    )
    return finish(
        info, rest, [panel_a, panel_b], linv, factor, pieces_a + pieces_b, layout, 1, coeffs
    )


def solution(mesh):
    in_specs = (P("rows", "cols"),)
    out_specs = (P("rows", "cols"), P(None, "cols"))
    return jax.shard_map(shards, mesh=mesh, in_specs=in_specs, out_specs=out_specs, check_vma=False)
```

```python
import jax
import jax.numpy as jnp
from jax import lax
from jax.experimental import pallas as pl
from jax.experimental.pallas import tpu as pltpu
from jax.sharding import PartitionSpec as P

PB = 512
NB = 128
F32 = jnp.float32
BF16 = jnp.bfloat16
HIGHEST = lax.Precision.HIGHEST
VMEM = pl.BlockSpec(memory_space=pltpu.VMEM)


ANY = pl.BlockSpec(memory_space=pl.ANY)
SMEM = pl.BlockSpec(memory_space=pltpu.SMEM)
TILE = 512
LIMITS = (4, 8, 6, 16)


def cost(flops):
    return pl.CostEstimate(flops=flops, bytes_accessed=1 << 20, transcendentals=0)


def vmem_limit(mib):
    return pltpu.CompilerParams(vmem_limit_bytes=mib << 20)


def mm(a, b, da, db, precision=None):
    return lax.dot_general(
        a, b, (((da,), (db,)), ((), ())), precision=precision, preferred_element_type=F32
    )


def split(x):
    high = x.astype(BF16)
    return high, (x - high.astype(F32)).astype(BF16)


def diag_block(d_ref, z_ref, f_ref):
    a_all = d_ref[...]
    row = lax.broadcasted_iota(jnp.int32, (NB, NB), 0)
    col = lax.broadcasted_iota(jnp.int32, (NB, NB), 1)
    z_all = jnp.where(row == col, 1.0, 0.0).astype(F32)
    lane = lax.broadcasted_iota(jnp.int32, (1, NB), 1)
    for j in range(0, NB, 4):
        base = (j // 8) * 8
        if a_all.shape[0] != NB - base:
            a_all, z_all = a_all[8:], z_all[8:]
        i, n = j - base, NB - base
        t = [a_all[i + k : i + k + 1, :] for k in range(4)]
        u = [z_all[i + k : i + k + 1, :] for k in range(4)]
        c = [jnp.broadcast_to(a_all[:, j + k : j + k + 1], (n, NB)) for k in range(4)]
        e = {
            (k, m): jnp.broadcast_to(t[k][:, j + m : j + m + 1], (1, NB))
            for k in range(4)
            for m in range(k, 4)
        }
        inv, low = [], {}
        for k in range(4):
            inv.append(1.0 / e[k, k])
            for m in range(k + 1, 4):
                low[m, k] = e[k, m] * inv[k]
            for m in range(k + 1, 4):
                for q in range(m, 4):
                    e[m, q] = e[m, q] - low[m, k] * e[k, q]
        for k in range(4):
            for m in range(k):
                t[k] = t[k] - low[k, m] * t[m]
                u[k] = u[k] - low[k, m] * u[m]
        x, y = [None] * 4, [None] * 4
        for k in reversed(range(4)):
            x[k], y[k] = t[k] * inv[k], u[k] * inv[k]
            for m in range(k + 1, 4):
                x[k] = x[k] - low[m, k] * x[m]
                y[k] = y[k] - low[m, k] * y[m]
        for k in range(4):
            root = lax.rsqrt(e[k, k])
            f_ref[j + k : j + k + 1, :] = jnp.where(lane >= j + k, t[k] * root, 0.0)
            z_ref[j + k : j + k + 1, :] = u[k] * root
        if j + 4 < NB:
            a_all = a_all - ((c[0] * x[0] + c[1] * x[1]) + (c[2] * x[2] + c[3] * x[3]))
            z_all = z_all - ((c[0] * y[0] + c[1] * y[1]) + (c[2] * y[2] + c[3] * y[3]))


def chol_part(info, first, last, pieces=None, places=None, state=None):
    fresh = pieces is not None
    arrays = pieces if fresh else state
    n = arrays[0].shape[1]
    nb = n // NB
    n_in = len(arrays)

    def kernel(info_ref, *refs):
        work, f_out, l_out = refs[n_in : n_in + 3]
        diag, zs, fs = refs[n_in + 3 :]
        if fresh:
            chips = n_in // 2
            for ref, (core, chip) in zip(refs, places):
                h = ref.shape[0]
                off = (info_ref[1] ^ core) * (h * chips) + (info_ref[2] ^ chip) * h
                work[pl.ds(pl.multiple_of(off, 8), h), :] = ref[...]
            f_out[...] = jnp.zeros_like(f_out)
            l_out[...] = jnp.zeros_like(l_out)

        def body(k, carry):
            o = pl.multiple_of(k * NB, NB)
            diag[...] = work[pl.ds(o, NB), pl.ds(o, NB)]
            diag_block(diag, zs, fs)
            for kk in range(first, last):

                @pl.when(k == kk)
                def _():
                    o, e = kk * NB, kk * NB + NB
                    z = zs[...]
                    f_out[o:e, o:e] = fs[...]
                    lk = z
                    if kk > 0:
                        lk = jnp.concatenate([mm(z, l_out[o:e, :o], 1, 0, HIGHEST), z], axis=1)
                    l_out[o:e, :e] = lk
                    if kk < nb - 1:
                        u = mm(z, work[o:e, e:], 1, 0, HIGHEST)
                        f_out[o:e, e:] = u
                        work[e:, e:] -= mm(u, u, 0, 0, HIGHEST)
                        l_out[e:, :e] -= mm(u, lk, 0, 0, HIGHEST)

            return carry

        lax.fori_loop(first, last, body, 0)

    shape = jax.ShapeDtypeStruct((n, n), F32)
    return pl.pallas_call(
        kernel,
        out_shape=(shape, shape, shape),
        in_specs=[SMEM] + [VMEM] * n_in,
        out_specs=(VMEM, VMEM, VMEM),
        scratch_shapes=[pltpu.VMEM((NB, NB), F32)] * 3,
        input_output_aliases={} if fresh else {1: 0, 2: 1, 3: 2},
        compiler_params=vmem_limit(LIMITS[2]),
        cost_estimate=cost(1),
        name="chol_part",
    )(info, *arrays)


def stage(snapshots):
    rows, cols = snapshots.shape

    def kernel(s_ref, h_ref, l_ref):
        for r in range(0, rows, 256):
            h_ref[r : r + 256, :], l_ref[r : r + 256, :] = split(s_ref[r : r + 256, :])

    return pl.pallas_call(
        kernel,
        out_shape=(jax.ShapeDtypeStruct((rows, cols), BF16),) * 2,
        in_specs=[VMEM],
        out_specs=(VMEM, VMEM),
        compiler_params=vmem_limit(LIMITS[0]),
        cost_estimate=cost(10**9),
        name="stage",
    )(snapshots)


def panel_dot(info, own, high, low, parts, size, first, width, scale, ready=None):
    rows, half = own.shape[0], PB // 2
    fresh = ready is None
    extra = [own, *parts] if fresh else [ready]
    n_extra = len(extra)
    tile = min(TILE, width)

    def kernel(info_ref, h_ref, l_ref, *rest):
        extra_refs, rest = rest[:n_extra], rest[n_extra:]
        send_ref, mine_ref = rest[:2]
        ms = rest[-1]
        pt = rest[3] if fresh else extra_refs[0]
        if fresh:
            p_ref = rest[2]

            @pl.when(info_ref[0] == 0)
            def _():
                p_ref[...] = extra_refs[0][...]

            if n_extra > 1:

                @pl.when(info_ref[0] != 0)
                def _():
                    for k, ref in enumerate(extra_refs[1:]):
                        start = pl.multiple_of(info_ref[3 + k], 8)
                        p_ref[pl.ds(start, size), :] = ref[...]

            def turn(i, carry):
                cut = pl.ds(pl.multiple_of(i * 256, 256), 256)
                ph, plow = split(p_ref[cut, :])
                pt[:PB, cut], pt[PB:, cut] = ph.T, plow.T
                return carry

            lax.fori_loop(0, rows // 256, turn, 0)

        def step(i, carry):
            cut = pl.ds(pl.multiple_of(i * tile, tile), tile)
            source = pl.ds(pl.multiple_of(first + i * tile, tile), tile)
            both = mm(pt[...], h_ref[:, source], 1, 0)
            ms[...] = (both[:PB] + (both[PB:] + mm(pt[:PB, :], l_ref[:, source], 1, 0))) * scale
            send_ref[:, cut] = ms[pl.ds(pl.multiple_of((1 - info_ref[1]) * half, half), half), :]
            mine_ref[:, cut] = ms[pl.ds(pl.multiple_of(info_ref[1] * half, half), half), :]
            return carry

        lax.fori_loop(0, width // tile, step, 0)

    out = [jax.ShapeDtypeStruct((half, width), F32)] * 2
    if fresh:
        out += [jax.ShapeDtypeStruct((rows, PB), F32), jax.ShapeDtypeStruct((2 * PB, rows), BF16)]
    return pl.pallas_call(
        kernel,
        out_shape=out,
        in_specs=[SMEM] + [VMEM] * (2 + n_extra),
        out_specs=[VMEM] * len(out),
        scratch_shapes=[pltpu.VMEM((PB, tile), F32)],
        compiler_params=vmem_limit(LIMITS[1]),
        cost_estimate=cost(6 * rows * PB * width),
        name="panel_dot",
    )(info, high, low, *extra)


def basis(panel, linv):
    rows = panel.shape[0]

    def kernel(p_ref, l_ref, b_ref, b3, l3):
        lh, ll = split(l_ref[...])
        l3[:, :PB], l3[:, PB : 2 * PB], l3[:, 2 * PB :] = lh, lh, ll

        def step(i, carry):
            cut = pl.ds(pl.multiple_of(i * 256, 256), 256)
            lh, ll = l3[:, :PB], l3[:, 2 * PB :]
            ph, plow = split(p_ref[cut, :])
            b = mm(ph, lh, 1, 1) + (mm(ph, ll, 1, 1) + mm(plow, lh, 1, 1))
            b_ref[cut, :] = b
            bh, bl = split(b)
            b3[cut, :PB], b3[cut, PB : 2 * PB], b3[cut, 2 * PB :] = bh, bh, bl
            return carry

        lax.fori_loop(0, rows // 256, step, 0)

    return pl.pallas_call(
        kernel,
        out_shape=(
            jax.ShapeDtypeStruct((rows, PB), F32),
            jax.ShapeDtypeStruct((rows, 3 * PB), BF16),
            jax.ShapeDtypeStruct((PB, 3 * PB), BF16),
        ),
        in_specs=[VMEM] * 2,
        out_specs=(VMEM,) * 3,
        compiler_params=vmem_limit(LIMITS[2]),
        cost_estimate=cost(6 * rows * PB * PB),
        name="basis",
    )(panel, linv)


def finish(info, snapshots, b, b3, l3, factor, pieces, places, first, width, done=None):
    rows, cols = snapshots.shape
    tile = min(TILE, width)
    n_pieces, chips = len(pieces), len(pieces) // 2
    later = [] if done is None else list(done)

    def kernel(info_ref, s_ref, b_ref, b3_ref, l3_ref, f_ref, *rest):
        m_refs, rest = rest[:n_pieces], rest[n_pieces + len(later) :]
        up_hbm, co_hbm, ms, m3, p3, up, co, sems = rest
        copies = []
        for t in range(width // tile):
            slot, cut = t % 2, pl.ds(t * tile, tile)
            goal = pl.ds(first + t * tile, tile)
            if t >= 2:
                for copy in copies[t - 2]:
                    copy.wait()
            for ref, (core, chip) in zip(m_refs, places):
                h = ref.shape[0]
                off = (info_ref[1] ^ core) * (h * chips) + (info_ref[2] ^ chip) * h
                ms[pl.ds(pl.multiple_of(off, 8), h), :] = ref[:, cut]
            mh, ml = split(ms[...])
            m3[:PB, :], m3[PB : 2 * PB, :], m3[2 * PB :, :] = mh, ml, mh
            proj = mm(l3_ref[...], m3[...], 1, 0)
            ph, plow = split(proj)
            p3[:PB, :], p3[PB : 2 * PB, :], p3[2 * PB :, :] = ph, plow, ph
            co[slot] = proj
            up[slot] = s_ref[:, goal] - mm(b3_ref[...], p3[...], 1, 0)
            if first + t * tile < PB:

                @pl.when(info_ref[0] == 0)
                def _():
                    co[slot] = f_ref[:, goal]
                    up[slot] = b_ref[:, goal]

            pair = (
                pltpu.make_async_copy(up.at[slot], up_hbm.at[:, goal], sems.at[0, slot]),
                pltpu.make_async_copy(co.at[slot], co_hbm.at[:, goal], sems.at[1, slot]),
            )
            for copy in pair:
                copy.start()
            copies.append(pair)
        for pair in copies[-2:]:
            for copy in pair:
                copy.wait()

    operands = [info, snapshots, b, b3, l3, factor, *pieces, *later]
    return pl.pallas_call(
        kernel,
        out_shape=(
            jax.ShapeDtypeStruct((rows, cols), F32),
            jax.ShapeDtypeStruct((PB, cols), F32),
        ),
        in_specs=[SMEM] + [VMEM] * (5 + n_pieces) + [ANY] * len(later),
        out_specs=(ANY, ANY),
        scratch_shapes=[
            pltpu.VMEM((PB, tile), F32),
            pltpu.VMEM((3 * PB, tile), BF16),
            pltpu.VMEM((3 * PB, tile), BF16),
            pltpu.VMEM((2, rows, tile), F32),
            pltpu.VMEM((2, PB, tile), F32),
            pltpu.SemaphoreType.DMA((2, 2)),
        ],
        input_output_aliases={len(operands) - 2: 0, len(operands) - 1: 1} if later else {},
        compiler_params=vmem_limit(LIMITS[3]),
        cost_estimate=cost(10**10),
        name="finish",
    )(*operands)


def part_size(rows, parts):
    return -(-rows // (8 * parts)) * 8


def spread_out(x, n):
    rows, parts = x.shape[0], n - 1
    size = part_size(rows, parts)
    got = []
    for k in reversed(range(parts)):
        start = min(k * size, rows - size)
        got.append(lax.ppermute(x[start : start + size], "cols", [(0, k + 1)]))
    return sum(got[1:], got[0])


def spread_round(mine, n):
    got, parts = [mine], n - 1
    for k in range(1, parts):
        pairs = [(1 + i, 1 + (i + k) % parts) for i in range(parts)]
        got.append(lax.ppermute(mine, "cols", pairs))
    return got


def after(x, *others):
    return lax.optimization_barrier((x, others))[0]


def swap(n, k):
    return [(i, i ^ k) for i in range(n)]


def take(a, start, size):
    return lax.dynamic_slice_in_dim(a, start, size, 0)


def join_cores(send, mine, n):
    return mine + lax.ppermute(send, "rows", swap(n, 1))


def scatter_chips(mine, n):
    chips = n // 2
    chip = lax.axis_index("rows") >> 1
    piece = mine.shape[0] // chips
    own = take(mine, chip * piece, piece)
    for k in range(1, chips):
        own = own + lax.ppermute(take(mine, (chip ^ k) * piece, piece), "rows", swap(n, 2 * k))
    return own


def gather_rows(own, n):
    got = [own] + [lax.ppermute(own, "rows", swap(n, 2 * k)) for k in range(1, n // 2)]
    other = [lax.ppermute(g, "rows", swap(n, 1)) for g in got]
    return got + other, [(0, k) for k in range(n // 2)] + [(1, k) for k in range(n // 2)]


def shards(snapshots):
    rows_dev, cols_dev = snapshots.shape
    n_rows, n_cols = lax.axis_size("rows"), lax.axis_size("cols")
    total_rows = rows_dev * n_rows
    z, index = lax.axis_index("cols"), lax.axis_index("rows")
    core = index & 1
    parts = n_cols - 1
    size = part_size(rows_dev, parts)
    starts = [jnp.minimum(((z - 1 - k) % parts) * size, rows_dev - size) for k in range(parts)]
    info = jnp.stack([z, core, index >> 1] + starts).astype(jnp.int32)
    half = PB // 2
    panel = snapshots[:, :PB]

    mine = spread_out(panel, n_cols)
    gram = mm(panel, panel, 0, 0, HIGHEST) / total_rows
    joined = join_cores(take(gram, (1 - core) * half, half), take(gram, core * half, half), n_rows)
    high, low = stage(after(snapshots, joined))
    share = scatter_chips(joined, n_rows)
    far = [lax.ppermute(share, "cols", [(0, k)]) for k in reversed(range(1, n_cols))]
    share = jnp.where(z == 0, share, sum(far, jnp.zeros_like(share)))
    grams, places = gather_rows(share, n_rows)
    got = spread_round(mine, n_cols)
    _, factor, linv = chol_part(info, 0, PB // NB, pieces=after(grams, mine, high), places=places)

    width = cols_dev // 2
    dot = lambda got, first, ready=None: panel_dot(
        info, panel, high, low, got, size, first, width, 1.0 / total_rows, ready
    )
    send, keep, whole, turned = dot(after(got, linv), 0)
    joined1 = join_cores(send, keep, n_rows)
    send, keep = dot(None, width, turned)
    joined2 = join_cores(send, keep, n_rows)
    own1 = scatter_chips(joined1, n_rows)
    own2 = scatter_chips(joined2, n_rows)
    b, b3, l3 = basis(after(whole, joined2), linv)
    pieces1, _ = gather_rows(own1, n_rows)
    pieces2, _ = gather_rows(own2, n_rows)
    done = finish(
        info, snapshots, b, b3, after(l3, own2), factor, pieces1, places, 0, width
    )
    return finish(info, snapshots, b, b3, l3, factor, pieces2, places, width, width, done)


def solution(mesh):
    in_specs = (P("rows", "cols"),)
    out_specs = (P("rows", "cols"), P(None, "cols"))
    return jax.shard_map(shards, mesh=mesh, in_specs=in_specs, out_specs=out_specs, check_vma=False)
```

```python
import jax
import jax.numpy as jnp
from jax import lax
from jax.experimental import pallas as pl
from jax.experimental.pallas import tpu as pltpu
from jax.sharding import PartitionSpec as P

PB = 512
NB = 128
F32 = jnp.float32
BF16 = jnp.bfloat16
HIGHEST = lax.Precision.HIGHEST
VMEM = pl.BlockSpec(memory_space=pltpu.VMEM)


ANY = pl.BlockSpec(memory_space=pl.ANY)
SMEM = pl.BlockSpec(memory_space=pltpu.SMEM)
TILE = 512
LIMITS = (4, 8, 6, 16)


def cost(flops):
    return pl.CostEstimate(flops=flops, bytes_accessed=1 << 20, transcendentals=0)


def vmem_limit(mib):
    return pltpu.CompilerParams(vmem_limit_bytes=mib << 20)


def mm(a, b, da, db, precision=None):
    return lax.dot_general(
        a, b, (((da,), (db,)), ((), ())), precision=precision, preferred_element_type=F32
    )


def split(x):
    high = x.astype(BF16)
    return high, (x - high.astype(F32)).astype(BF16)


def diag_block(d_ref, z_ref, f_ref):
    a_all = d_ref[...]
    row = lax.broadcasted_iota(jnp.int32, (NB, NB), 0)
    col = lax.broadcasted_iota(jnp.int32, (NB, NB), 1)
    z_all = jnp.where(row == col, 1.0, 0.0).astype(F32)
    lane = lax.broadcasted_iota(jnp.int32, (1, NB), 1)
    for j in range(0, NB, 4):
        base = (j // 8) * 8
        if a_all.shape[0] != NB - base:
            a_all, z_all = a_all[8:], z_all[8:]
        i, n = j - base, NB - base
        t = [a_all[i + k : i + k + 1, :] for k in range(4)]
        u = [z_all[i + k : i + k + 1, :] for k in range(4)]
        c = [jnp.broadcast_to(a_all[:, j + k : j + k + 1], (n, NB)) for k in range(4)]
        e = {
            (k, m): jnp.broadcast_to(t[k][:, j + m : j + m + 1], (1, NB))
            for k in range(4)
            for m in range(k, 4)
        }
        inv, low = [], {}
        for k in range(4):
            inv.append(1.0 / e[k, k])
            for m in range(k + 1, 4):
                low[m, k] = e[k, m] * inv[k]
            for m in range(k + 1, 4):
                for q in range(m, 4):
                    e[m, q] = e[m, q] - low[m, k] * e[k, q]
        for k in range(4):
            for m in range(k):
                t[k] = t[k] - low[k, m] * t[m]
                u[k] = u[k] - low[k, m] * u[m]
        x, y = [None] * 4, [None] * 4
        for k in reversed(range(4)):
            x[k], y[k] = t[k] * inv[k], u[k] * inv[k]
            for m in range(k + 1, 4):
                x[k] = x[k] - low[m, k] * x[m]
                y[k] = y[k] - low[m, k] * y[m]
        for k in range(4):
            root = lax.rsqrt(e[k, k])
            f_ref[j + k : j + k + 1, :] = jnp.where(lane >= j + k, t[k] * root, 0.0)
            z_ref[j + k : j + k + 1, :] = u[k] * root
        if j + 4 < NB:
            a_all = a_all - ((c[0] * x[0] + c[1] * x[1]) + (c[2] * x[2] + c[3] * x[3]))
            z_all = z_all - ((c[0] * y[0] + c[1] * y[1]) + (c[2] * y[2] + c[3] * y[3]))


def chol_part(info, first, last, pieces=None, places=None, state=None):
    fresh = pieces is not None
    arrays = pieces if fresh else state
    n = arrays[0].shape[1]
    nb = n // NB
    n_in = len(arrays)

    def kernel(info_ref, *refs):
        work, f_out, l_out = refs[n_in : n_in + 3]
        diag, zs, fs = refs[n_in + 3 :]
        if fresh:
            chips = n_in // 2
            for ref, (core, chip) in zip(refs, places):
                h = ref.shape[0]
                off = (info_ref[1] ^ core) * (h * chips) + (info_ref[2] ^ chip) * h
                work[pl.ds(pl.multiple_of(off, 8), h), :] = ref[...]
            f_out[...] = jnp.zeros_like(f_out)
            l_out[...] = jnp.zeros_like(l_out)

        def body(k, carry):
            o = pl.multiple_of(k * NB, NB)
            diag[...] = work[pl.ds(o, NB), pl.ds(o, NB)]
            diag_block(diag, zs, fs)
            for kk in range(first, last):

                @pl.when(k == kk)
                def _():
                    o, e = kk * NB, kk * NB + NB
                    z = zs[...]
                    f_out[o:e, o:e] = fs[...]
                    lk = z
                    if kk > 0:
                        lk = jnp.concatenate([mm(z, l_out[o:e, :o], 1, 0, HIGHEST), z], axis=1)
                    l_out[o:e, :e] = lk
                    if kk < nb - 1:
                        u = mm(z, work[o:e, e:], 1, 0, HIGHEST)
                        f_out[o:e, e:] = u
                        work[e:, e:] -= mm(u, u, 0, 0, HIGHEST)
                        l_out[e:, :e] -= mm(u, lk, 0, 0, HIGHEST)

            return carry

        lax.fori_loop(first, last, body, 0)

    shape = jax.ShapeDtypeStruct((n, n), F32)
    return pl.pallas_call(
        kernel,
        out_shape=(shape, shape, shape),
        in_specs=[SMEM] + [VMEM] * n_in,
        out_specs=(VMEM, VMEM, VMEM),
        scratch_shapes=[pltpu.VMEM((NB, NB), F32)] * 3,
        input_output_aliases={} if fresh else {1: 0, 2: 1, 3: 2},
        compiler_params=vmem_limit(LIMITS[2]),
        cost_estimate=cost((last - first) * 8 * 10**9),
        name="chol_part",
    )(info, *arrays)


def stage(snapshots):
    rows, cols = snapshots.shape

    def kernel(s_ref, h_ref, l_ref):
        for r in range(0, rows, 256):
            h_ref[r : r + 256, :], l_ref[r : r + 256, :] = split(s_ref[r : r + 256, :])

    return pl.pallas_call(
        kernel,
        out_shape=(jax.ShapeDtypeStruct((rows, cols), BF16),) * 2,
        in_specs=[VMEM],
        out_specs=(VMEM, VMEM),
        compiler_params=vmem_limit(LIMITS[0]),
        cost_estimate=cost(10**9),
        name="stage",
    )(snapshots)


def basis(panels, linv):
    rows, n_panels = panels[0].shape[0], len(panels)

    def kernel(*refs):
        p_refs, (l_ref, b_ref, b3, l3) = refs[:n_panels], refs[n_panels:]
        lh, ll = split(l_ref[...])
        l3[:, :PB], l3[:, PB : 2 * PB], l3[:, 2 * PB :] = lh, lh, ll

        def step(i, carry):
            cut = pl.ds(pl.multiple_of(i * 256, 256), 256)
            lh, ll = l3[:, :PB], l3[:, 2 * PB :]
            ph, plow = split(jnp.concatenate([p[cut, :] for p in p_refs], axis=1))
            b = mm(ph, lh, 1, 1) + (mm(ph, ll, 1, 1) + mm(plow, lh, 1, 1))
            b_ref[cut, :] = b
            bh, bl = split(b)
            b3[cut, :PB], b3[cut, PB : 2 * PB], b3[cut, 2 * PB :] = bh, bh, bl
            return carry

        lax.fori_loop(0, rows // 256, step, 0)

    return pl.pallas_call(
        kernel,
        out_shape=(
            jax.ShapeDtypeStruct((rows, PB), F32),
            jax.ShapeDtypeStruct((rows, 3 * PB), BF16),
            jax.ShapeDtypeStruct((PB, 3 * PB), BF16),
        ),
        in_specs=[VMEM] * (n_panels + 1),
        out_specs=(VMEM,) * 3,
        compiler_params=vmem_limit(LIMITS[2]),
        cost_estimate=cost(6 * rows * PB * PB),
        name="basis",
    )(*panels, linv)


def finish(info, snapshots, b, b3, l3, factor, pieces, layout):
    rows, cols = snapshots.shape
    tile = min(TILE, cols)
    n_pieces = len(pieces)
    chips = 1 + max(chip for _, _, chip in layout)

    def kernel(info_ref, s_ref, b_ref, b3_ref, l3_ref, f_ref, *rest):
        m_refs = rest[:n_pieces]
        up_hbm, co_hbm, ms, m3, p3, up, co, sems = rest[n_pieces:]
        copies = []
        for t in range(cols // tile):
            slot, cut = t % 2, pl.ds(t * tile, tile)
            if t >= 2:
                for copy in copies[t - 2]:
                    copy.wait()
            for ref, (base, core, chip) in zip(m_refs, layout):
                h = ref.shape[0]
                off = base + (info_ref[1] ^ core) * (h * chips) + (info_ref[2] ^ chip) * h
                ms[pl.ds(pl.multiple_of(off, 8), h), :] = ref[:, cut]
            mh, ml = split(ms[...])
            m3[:PB, :], m3[PB : 2 * PB, :], m3[2 * PB :, :] = mh, ml, mh
            proj = mm(l3_ref[...], m3[...], 1, 0)
            ph, plow = split(proj)
            p3[:PB, :], p3[PB : 2 * PB, :], p3[2 * PB :, :] = ph, plow, ph
            co[slot] = proj
            up[slot] = s_ref[:, cut] - mm(b3_ref[...], p3[...], 1, 0)
            if t * tile < PB:

                @pl.when(info_ref[0] == 0)
                def _():
                    co[slot] = f_ref[:, cut]
                    up[slot] = b_ref[:, cut]

            pair = (
                pltpu.make_async_copy(up.at[slot], up_hbm.at[:, cut], sems.at[0, slot]),
                pltpu.make_async_copy(co.at[slot], co_hbm.at[:, cut], sems.at[1, slot]),
            )
            for copy in pair:
                copy.start()
            copies.append(pair)
        for pair in copies[-2:]:
            for copy in pair:
                copy.wait()

    return pl.pallas_call(
        kernel,
        out_shape=(
            jax.ShapeDtypeStruct((rows, cols), F32),
            jax.ShapeDtypeStruct((PB, cols), F32),
        ),
        in_specs=[SMEM] + [VMEM] * (5 + n_pieces),
        out_specs=(ANY, ANY),
        scratch_shapes=[
            pltpu.VMEM((PB, tile), F32),
            pltpu.VMEM((3 * PB, tile), BF16),
            pltpu.VMEM((3 * PB, tile), BF16),
            pltpu.VMEM((2, rows, tile), F32),
            pltpu.VMEM((2, PB, tile), F32),
            pltpu.SemaphoreType.DMA((2, 2)),
        ],
        compiler_params=vmem_limit(LIMITS[3]),
        cost_estimate=cost(10**10),
        name="finish",
    )(info, snapshots, b, b3, l3, factor, *pieces)


def panel_dot(info, own, high, low, parts, size, scale):
    rows, width = own.shape
    cols, half = high.shape[1], width // 2
    n_parts = len(parts)
    tile = min(TILE, cols)

    def kernel(info_ref, h_ref, l_ref, own_ref, *rest):
        part_refs = rest[:n_parts]
        send_ref, mine_ref, p_ref, pt, ms = rest[n_parts:]

        @pl.when(info_ref[0] == 0)
        def _():
            p_ref[...] = own_ref[...]

        if n_parts:

            @pl.when(info_ref[0] != 0)
            def _():
                for k, ref in enumerate(part_refs):
                    start = pl.multiple_of(info_ref[3 + k], 8)
                    p_ref[pl.ds(start, size), :] = ref[...]

        for r in range(0, rows, 256):
            ph, plow = split(p_ref[r : r + 256, :])
            pt[:width, r : r + 256], pt[width:, r : r + 256] = ph.T, plow.T

        def step(i, carry):
            cut = pl.ds(pl.multiple_of(i * tile, tile), tile)
            both = mm(pt[...], h_ref[:, cut], 1, 0)
            ms[...] = (both[:width] + (both[width:] + mm(pt[:width, :], l_ref[:, cut], 1, 0))) * scale
            send_ref[:, cut] = ms[pl.ds(pl.multiple_of((1 - info_ref[1]) * half, half), half), :]
            mine_ref[:, cut] = ms[pl.ds(pl.multiple_of(info_ref[1] * half, half), half), :]
            return carry

        lax.fori_loop(0, cols // tile, step, 0)

    out = jax.ShapeDtypeStruct((half, cols), F32)
    return pl.pallas_call(
        kernel,
        out_shape=(out, out, jax.ShapeDtypeStruct((rows, width), F32)),
        in_specs=[SMEM] + [VMEM] * (3 + n_parts),
        out_specs=(VMEM, VMEM, VMEM),
        scratch_shapes=[
            pltpu.VMEM((2 * width, rows), BF16),
            pltpu.VMEM((width, tile), F32),
        ],
        compiler_params=vmem_limit(LIMITS[1]),
        cost_estimate=cost(6 * rows * cols * width),
        name="panel_dot",
    )(info, high, low, own, *parts)


def part_size(rows, parts):
    return -(-rows // (8 * parts)) * 8


def spread_out(x, n):
    rows, parts = x.shape[0], n - 1
    size = part_size(rows, parts)
    got = []
    for k in reversed(range(parts)):
        start = min(k * size, rows - size)
        got.append(lax.ppermute(x[start : start + size], "cols", [(0, k + 1)]))
    return sum(got[1:], got[0])


def spread_round(mine, n):
    got, parts = [mine], n - 1
    for k in range(1, parts):
        pairs = [(1 + i, 1 + (i + k) % parts) for i in range(parts)]
        got.append(lax.ppermute(mine, "cols", pairs))
    return got


def after(x, *others):
    return lax.optimization_barrier((x, others))[0]


def swap(n, k):
    return [(i, i ^ k) for i in range(n)]


def take(a, start, size):
    return lax.dynamic_slice_in_dim(a, start, size, 0)


def join_cores(send, mine, n):
    return mine + lax.ppermute(send, "rows", swap(n, 1))


def scatter_chips(mine, n):
    chips = n // 2
    chip = lax.axis_index("rows") >> 1
    piece = mine.shape[0] // chips
    own = take(mine, chip * piece, piece)
    for k in range(1, chips):
        own = own + lax.ppermute(take(mine, (chip ^ k) * piece, piece), "rows", swap(n, 2 * k))
    return own


def gather_rows(own, n):
    got = [own] + [lax.ppermute(own, "rows", swap(n, 2 * k)) for k in range(1, n // 2)]
    other = [lax.ppermute(g, "rows", swap(n, 1)) for g in got]
    return got + other, [(0, k) for k in range(n // 2)] + [(1, k) for k in range(n // 2)]


def shards(snapshots):
    rows_dev, cols_dev = snapshots.shape
    n_rows, n_cols = lax.axis_size("rows"), lax.axis_size("cols")
    total_rows = rows_dev * n_rows
    z, index = lax.axis_index("cols"), lax.axis_index("rows")
    core = index & 1
    parts = n_cols - 1
    size = part_size(rows_dev, parts)
    starts = [jnp.minimum(((z - 1 - k) % parts) * size, rows_dev - size) for k in range(parts)]
    info = jnp.stack([z, core, index >> 1] + starts).astype(jnp.int32)
    half = PB // 2
    panel = snapshots[:, :PB]

    dot = lambda got, base: panel_dot(
        info, panel[:, base : base + half], high, low, got, size, 1.0 / total_rows
    )

    mine_a = spread_out(panel[:, :half], n_cols)
    gram = mm(panel, panel, 0, 0, HIGHEST) / total_rows
    joined = join_cores(take(gram, (1 - core) * half, half), take(gram, core * half, half), n_rows)
    high, low = stage(snapshots)
    share = scatter_chips(joined, n_rows)
    far = [lax.ppermute(share, "cols", [(0, k)]) for k in reversed(range(1, n_cols))]
    got_a = spread_round(mine_a, n_cols)
    mine_b = spread_out(after(panel[:, half:], got_a), n_cols)
    share = jnp.where(z == 0, share, sum(far, jnp.zeros_like(share)))
    grams, places = gather_rows(share, n_rows)

    send, keep, panel_a = dot(after(got_a, far, high), 0)
    joined = join_cores(send, keep, n_rows)
    got_b = spread_round(mine_b, n_cols)
    own_a = scatter_chips(joined, n_rows)
    state = chol_part(info, 0, 2, pieces=after(grams, joined, mine_b), places=places)
    pieces_a, where = gather_rows(own_a, n_rows)
    send, keep, panel_b = dot(after(got_b, own_a, state), half)
    joined = join_cores(send, keep, n_rows)
    own_b = scatter_chips(joined, n_rows)
    state = chol_part(info, 2, 3, state=after(state, joined))
    pieces_b, _ = gather_rows(after(own_b, state), n_rows)
    _, factor, linv = chol_part(info, 3, 4, state=after(state, own_b))
    b, b3, l3 = basis([panel_a, panel_b], linv)
    layout = [(base,) + w for base in (0, half) for w in where]
    return finish(info, snapshots, b, b3, l3, factor, pieces_a + pieces_b, layout)


def solution(mesh):
    in_specs = (P("rows", "cols"),)
    out_specs = (P("rows", "cols"), P(None, "cols"))
    return jax.shard_map(shards, mesh=mesh, in_specs=in_specs, out_specs=out_specs, check_vma=False)
```

```python
import jax
import jax.numpy as jnp
from jax import lax
from jax.experimental import pallas as pl
from jax.experimental.pallas import tpu as pltpu
from jax.sharding import PartitionSpec as P

PB = 512
NB = 128
F32 = jnp.float32
BF16 = jnp.bfloat16
HIGHEST = lax.Precision.HIGHEST
VMEM = pl.BlockSpec(memory_space=pltpu.VMEM)


ANY = pl.BlockSpec(memory_space=pl.ANY)
SMEM = pl.BlockSpec(memory_space=pltpu.SMEM)
TILE = 512
LIMITS = (4, 8, 6, 16)


def cost(flops):
    return pl.CostEstimate(flops=flops, bytes_accessed=1 << 20, transcendentals=0)


def vmem_limit(mib):
    return pltpu.CompilerParams(vmem_limit_bytes=mib << 20)


def mm(a, b, da, db, precision=None):
    return lax.dot_general(
        a, b, (((da,), (db,)), ((), ())), precision=precision, preferred_element_type=F32
    )


def split(x):
    high = x.astype(BF16)
    return high, (x - high.astype(F32)).astype(BF16)


def diag_block(d_ref, z_ref, f_ref):
    a_all = d_ref[...]
    row = lax.broadcasted_iota(jnp.int32, (NB, NB), 0)
    col = lax.broadcasted_iota(jnp.int32, (NB, NB), 1)
    z_all = jnp.where(row == col, 1.0, 0.0).astype(F32)
    lane = lax.broadcasted_iota(jnp.int32, (1, NB), 1)
    for j in range(0, NB, 4):
        base = (j // 8) * 8
        if a_all.shape[0] != NB - base:
            a_all, z_all = a_all[8:], z_all[8:]
        i, n = j - base, NB - base
        t = [a_all[i + k : i + k + 1, :] for k in range(4)]
        u = [z_all[i + k : i + k + 1, :] for k in range(4)]
        c = [jnp.broadcast_to(a_all[:, j + k : j + k + 1], (n, NB)) for k in range(4)]
        e = {
            (k, m): jnp.broadcast_to(t[k][:, j + m : j + m + 1], (1, NB))
            for k in range(4)
            for m in range(k, 4)
        }
        inv, low = [], {}
        for k in range(4):
            inv.append(1.0 / e[k, k])
            for m in range(k + 1, 4):
                low[m, k] = e[k, m] * inv[k]
            for m in range(k + 1, 4):
                for q in range(m, 4):
                    e[m, q] = e[m, q] - low[m, k] * e[k, q]
        for k in range(4):
            for m in range(k):
                t[k] = t[k] - low[k, m] * t[m]
                u[k] = u[k] - low[k, m] * u[m]
        x, y = [None] * 4, [None] * 4
        for k in reversed(range(4)):
            x[k], y[k] = t[k] * inv[k], u[k] * inv[k]
            for m in range(k + 1, 4):
                x[k] = x[k] - low[m, k] * x[m]
                y[k] = y[k] - low[m, k] * y[m]
        for k in range(4):
            root = lax.rsqrt(e[k, k])
            f_ref[j + k : j + k + 1, :] = jnp.where(lane >= j + k, t[k] * root, 0.0)
            z_ref[j + k : j + k + 1, :] = u[k] * root
        if j + 4 < NB:
            a_all = a_all - ((c[0] * x[0] + c[1] * x[1]) + (c[2] * x[2] + c[3] * x[3]))
            z_all = z_all - ((c[0] * y[0] + c[1] * y[1]) + (c[2] * y[2] + c[3] * y[3]))


def chol_part(info, first, last, pieces=None, places=None, state=None):
    fresh = pieces is not None
    arrays = pieces if fresh else state
    n = arrays[0].shape[1]
    nb = n // NB
    n_in = len(arrays)

    def kernel(info_ref, *refs):
        work, f_out, l_out = refs[n_in : n_in + 3]
        diag, zs, fs = refs[n_in + 3 :]
        if fresh:
            chips = n_in // 2
            for ref, (core, chip) in zip(refs, places):
                h = ref.shape[0]
                off = (info_ref[1] ^ core) * (h * chips) + (info_ref[2] ^ chip) * h
                work[pl.ds(pl.multiple_of(off, 8), h), :] = ref[...]
            f_out[...] = jnp.zeros_like(f_out)
            l_out[...] = jnp.zeros_like(l_out)

        def body(k, carry):
            o = pl.multiple_of(k * NB, NB)
            diag[...] = work[pl.ds(o, NB), pl.ds(o, NB)]
            diag_block(diag, zs, fs)
            for kk in range(first, last):

                @pl.when(k == kk)
                def _():
                    o, e = kk * NB, kk * NB + NB
                    z = zs[...]
                    f_out[o:e, o:e] = fs[...]
                    lk = z
                    if kk > 0:
                        lk = jnp.concatenate([mm(z, l_out[o:e, :o], 1, 0, HIGHEST), z], axis=1)
                    l_out[o:e, :e] = lk
                    if kk < nb - 1:
                        u = mm(z, work[o:e, e:], 1, 0, HIGHEST)
                        f_out[o:e, e:] = u
                        work[e:, e:] -= mm(u, u, 0, 0, HIGHEST)
                        l_out[e:, :e] -= mm(u, lk, 0, 0, HIGHEST)

            return carry

        lax.fori_loop(first, last, body, 0)

    shape = jax.ShapeDtypeStruct((n, n), F32)
    return pl.pallas_call(
        kernel,
        out_shape=(shape, shape, shape),
        in_specs=[SMEM] + [VMEM] * n_in,
        out_specs=(VMEM, VMEM, VMEM),
        scratch_shapes=[pltpu.VMEM((NB, NB), F32)] * 3,
        input_output_aliases={} if fresh else {1: 0, 2: 1, 3: 2},
        compiler_params=vmem_limit(LIMITS[2]),
        cost_estimate=cost((last - first) * 8 * 10**9),
        name="chol_part",
    )(info, *arrays)


def stage(snapshots):
    rows, cols = snapshots.shape

    def kernel(s_ref, h_ref, l_ref):
        for r in range(0, rows, 256):
            h_ref[r : r + 256, :], l_ref[r : r + 256, :] = split(s_ref[r : r + 256, :])

    return pl.pallas_call(
        kernel,
        out_shape=(jax.ShapeDtypeStruct((rows, cols), BF16),) * 2,
        in_specs=[VMEM],
        out_specs=(VMEM, VMEM),
        compiler_params=vmem_limit(LIMITS[0]),
        cost_estimate=cost(10**9),
        name="stage",
    )(snapshots)


def basis(panels, linv):
    rows, n_panels = panels[0].shape[0], len(panels)

    def kernel(*refs):
        p_refs, (l_ref, b_ref, b3, l3) = refs[:n_panels], refs[n_panels:]
        lh, ll = split(l_ref[...])
        l3[:, :PB], l3[:, PB : 2 * PB], l3[:, 2 * PB :] = lh, lh, ll

        def step(i, carry):
            cut = pl.ds(pl.multiple_of(i * 256, 256), 256)
            lh, ll = l3[:, :PB], l3[:, 2 * PB :]
            ph, plow = split(jnp.concatenate([p[cut, :] for p in p_refs], axis=1))
            b = mm(ph, lh, 1, 1) + (mm(ph, ll, 1, 1) + mm(plow, lh, 1, 1))
            b_ref[cut, :] = b
            bh, bl = split(b)
            b3[cut, :PB], b3[cut, PB : 2 * PB], b3[cut, 2 * PB :] = bh, bh, bl
            return carry

        lax.fori_loop(0, rows // 256, step, 0)

    return pl.pallas_call(
        kernel,
        out_shape=(
            jax.ShapeDtypeStruct((rows, PB), F32),
            jax.ShapeDtypeStruct((rows, 3 * PB), BF16),
            jax.ShapeDtypeStruct((PB, 3 * PB), BF16),
        ),
        in_specs=[VMEM] * (n_panels + 1),
        out_specs=(VMEM,) * 3,
        compiler_params=vmem_limit(LIMITS[2]),
        cost_estimate=cost(6 * rows * PB * PB),
        name="basis",
    )(*panels, linv)


def finish(info, snapshots, b, b3, l3, factor, pieces, layout):
    rows, cols = snapshots.shape
    tile = min(TILE, cols)
    n_pieces = len(pieces)
    chips = 1 + max(chip for _, _, chip in layout)

    def kernel(info_ref, s_ref, b_ref, b3_ref, l3_ref, f_ref, *rest):
        m_refs = rest[:n_pieces]
        up_hbm, co_hbm, ms, m3, p3, up, co, sems = rest[n_pieces:]
        copies = []
        for t in range(cols // tile):
            slot, cut = t % 2, pl.ds(t * tile, tile)
            if t >= 2:
                for copy in copies[t - 2]:
                    copy.wait()
            for ref, (base, core, chip) in zip(m_refs, layout):
                h = ref.shape[0]
                off = base + (info_ref[1] ^ core) * (h * chips) + (info_ref[2] ^ chip) * h
                ms[pl.ds(pl.multiple_of(off, 8), h), :] = ref[:, cut]
            mh, ml = split(ms[...])
            m3[:PB, :], m3[PB : 2 * PB, :], m3[2 * PB :, :] = mh, ml, mh
            proj = mm(l3_ref[...], m3[...], 1, 0)
            ph, plow = split(proj)
            p3[:PB, :], p3[PB : 2 * PB, :], p3[2 * PB :, :] = ph, plow, ph
            co[slot] = proj
            up[slot] = s_ref[:, cut] - mm(b3_ref[...], p3[...], 1, 0)
            if t * tile < PB:

                @pl.when(info_ref[0] == 0)
                def _():
                    co[slot] = f_ref[:, cut]
                    up[slot] = b_ref[:, cut]

            pair = (
                pltpu.make_async_copy(up.at[slot], up_hbm.at[:, cut], sems.at[0, slot]),
                pltpu.make_async_copy(co.at[slot], co_hbm.at[:, cut], sems.at[1, slot]),
            )
            for copy in pair:
                copy.start()
            copies.append(pair)
        for pair in copies[-2:]:
            for copy in pair:
                copy.wait()

    return pl.pallas_call(
        kernel,
        out_shape=(
            jax.ShapeDtypeStruct((rows, cols), F32),
            jax.ShapeDtypeStruct((PB, cols), F32),
        ),
        in_specs=[SMEM] + [VMEM] * (5 + n_pieces),
        out_specs=(ANY, ANY),
        scratch_shapes=[
            pltpu.VMEM((PB, tile), F32),
            pltpu.VMEM((3 * PB, tile), BF16),
            pltpu.VMEM((3 * PB, tile), BF16),
            pltpu.VMEM((2, rows, tile), F32),
            pltpu.VMEM((2, PB, tile), F32),
            pltpu.SemaphoreType.DMA((2, 2)),
        ],
        compiler_params=vmem_limit(LIMITS[3]),
        cost_estimate=cost(10**10),
        name="finish",
    )(info, snapshots, b, b3, l3, factor, *pieces)


def panel_dot(info, own, high, low, parts, size, scale):
    rows, width = own.shape
    cols, half = high.shape[1], width // 2
    n_parts = len(parts)
    tile = min(TILE, cols)

    def kernel(info_ref, h_ref, l_ref, own_ref, *rest):
        part_refs = rest[:n_parts]
        send_ref, mine_ref, p_ref, pt, ms = rest[n_parts:]

        @pl.when(info_ref[0] == 0)
        def _():
            p_ref[...] = own_ref[...]

        if n_parts:

            @pl.when(info_ref[0] != 0)
            def _():
                for k, ref in enumerate(part_refs):
                    start = pl.multiple_of(info_ref[3 + k], 8)
                    p_ref[pl.ds(start, size), :] = ref[...]

        for r in range(0, rows, 256):
            ph, plow = split(p_ref[r : r + 256, :])
            pt[:width, r : r + 256], pt[width:, r : r + 256] = ph.T, plow.T

        def step(i, carry):
            cut = pl.ds(pl.multiple_of(i * tile, tile), tile)
            both = mm(pt[...], h_ref[:, cut], 1, 0)
            ms[...] = (both[:width] + (both[width:] + mm(pt[:width, :], l_ref[:, cut], 1, 0))) * scale
            send_ref[:, cut] = ms[pl.ds(pl.multiple_of((1 - info_ref[1]) * half, half), half), :]
            mine_ref[:, cut] = ms[pl.ds(pl.multiple_of(info_ref[1] * half, half), half), :]
            return carry

        lax.fori_loop(0, cols // tile, step, 0)

    out = jax.ShapeDtypeStruct((half, cols), F32)
    return pl.pallas_call(
        kernel,
        out_shape=(out, out, jax.ShapeDtypeStruct((rows, width), F32)),
        in_specs=[SMEM] + [VMEM] * (3 + n_parts),
        out_specs=(VMEM, VMEM, VMEM),
        scratch_shapes=[
            pltpu.VMEM((2 * width, rows), BF16),
            pltpu.VMEM((width, tile), F32),
        ],
        compiler_params=vmem_limit(LIMITS[1]),
        cost_estimate=cost(6 * rows * cols * width),
        name="panel_dot",
    )(info, high, low, own, *parts)


def part_size(rows, parts):
    return -(-rows // (8 * parts)) * 8


def spread_out(x, n):
    rows, parts = x.shape[0], n - 1
    size = part_size(rows, parts)
    got = []
    for k in reversed(range(parts)):
        start = min(k * size, rows - size)
        got.append(lax.ppermute(x[start : start + size], "cols", [(0, k + 1)]))
    return sum(got[1:], got[0])


def spread_round(mine, n):
    got, parts = [mine], n - 1
    for k in range(1, parts):
        pairs = [(1 + i, 1 + (i + k) % parts) for i in range(parts)]
        got.append(lax.ppermute(mine, "cols", pairs))
    return got


def after(x, *others):
    return lax.optimization_barrier((x, others))[0]


def swap(n, k):
    return [(i, i ^ k) for i in range(n)]


def take(a, start, size):
    return lax.dynamic_slice_in_dim(a, start, size, 0)


def join_cores(send, mine, n):
    return mine + lax.ppermute(send, "rows", swap(n, 1))


def scatter_chips(mine, n):
    chips = n // 2
    chip = lax.axis_index("rows") >> 1
    piece = mine.shape[0] // chips
    own = take(mine, chip * piece, piece)
    for k in range(1, chips):
        own = own + lax.ppermute(take(mine, (chip ^ k) * piece, piece), "rows", swap(n, 2 * k))
    return own


def gather_rows(own, n):
    got = [own] + [lax.ppermute(own, "rows", swap(n, 2 * k)) for k in range(1, n // 2)]
    other = [lax.ppermute(g, "rows", swap(n, 1)) for g in got]
    return got + other, [(0, k) for k in range(n // 2)] + [(1, k) for k in range(n // 2)]


def shards(snapshots):
    rows_dev, cols_dev = snapshots.shape
    n_rows, n_cols = lax.axis_size("rows"), lax.axis_size("cols")
    total_rows = rows_dev * n_rows
    z, index = lax.axis_index("cols"), lax.axis_index("rows")
    core = index & 1
    parts = n_cols - 1
    size = part_size(rows_dev, parts)
    starts = [jnp.minimum(((z - 1 - k) % parts) * size, rows_dev - size) for k in range(parts)]
    info = jnp.stack([z, core, index >> 1] + starts).astype(jnp.int32)
    half = PB // 2
    panel = snapshots[:, :PB]

    dot = lambda got, base: panel_dot(
        info, panel[:, base : base + half], high, low, got, size, 1.0 / total_rows
    )

    mine_a = spread_out(panel[:, :half], n_cols)
    gram = mm(panel, panel, 0, 0, HIGHEST) / total_rows
    joined = join_cores(take(gram, (1 - core) * half, half), take(gram, core * half, half), n_rows)
    high, low = stage(snapshots)
    share = scatter_chips(joined, n_rows)
    far = [lax.ppermute(share, "cols", [(0, k)]) for k in reversed(range(1, n_cols))]
    got_a = spread_round(mine_a, n_cols)
    mine_b = spread_out(after(panel[:, half:], mine_a), n_cols)
    share = jnp.where(z == 0, share, sum(far, jnp.zeros_like(share)))
    grams, places = gather_rows(share, n_rows)

    send, keep, panel_a = dot(after(got_a, far, mine_b, high), 0)
    joined = join_cores(send, keep, n_rows)
    got_b = spread_round(mine_b, n_cols)
    own_a = scatter_chips(joined, n_rows)
    state = chol_part(info, 0, 2, pieces=after(grams, joined, mine_b), places=places)
    pieces_a, where = gather_rows(own_a, n_rows)
    send, keep, panel_b = dot(after(got_b, own_a, state), half)
    joined = join_cores(send, keep, n_rows)
    own_b = scatter_chips(joined, n_rows)
    _, factor, linv = chol_part(info, 2, 4, state=after(state, joined))
    pieces_b, _ = gather_rows(after(own_b, linv), n_rows)
    b, b3, l3 = basis([panel_a, panel_b], linv)
    layout = [(base,) + w for base in (0, half) for w in where]
    return finish(info, snapshots, b, b3, l3, factor, pieces_a + pieces_b, layout)


def solution(mesh):
    in_specs = (P("rows", "cols"),)
    out_specs = (P("rows", "cols"), P(None, "cols"))
    return jax.shard_map(shards, mesh=mesh, in_specs=in_specs, out_specs=out_specs, check_vma=False)
```

```python
import jax
import jax.numpy as jnp
from jax import lax
from jax.experimental import pallas as pl
from jax.experimental.pallas import tpu as pltpu
from jax.sharding import PartitionSpec as P

PB = 512
NB = 128
F32 = jnp.float32
BF16 = jnp.bfloat16
HIGHEST = lax.Precision.HIGHEST
VMEM = pl.BlockSpec(memory_space=pltpu.VMEM)


ANY = pl.BlockSpec(memory_space=pl.ANY)
SMEM = pl.BlockSpec(memory_space=pltpu.SMEM)
TILE = 512
LIMITS = (4, 8, 6, 16)


def cost(flops):
    return pl.CostEstimate(flops=flops, bytes_accessed=1 << 20, transcendentals=0)


def vmem_limit(mib):
    return pltpu.CompilerParams(vmem_limit_bytes=mib << 20)


def mm(a, b, da, db, precision=None):
    return lax.dot_general(
        a, b, (((da,), (db,)), ((), ())), precision=precision, preferred_element_type=F32
    )


def split(x):
    high = x.astype(BF16)
    return high, (x - high.astype(F32)).astype(BF16)


def diag_block(d_ref, z_ref, f_ref):
    a_all = d_ref[...]
    row = lax.broadcasted_iota(jnp.int32, (NB, NB), 0)
    col = lax.broadcasted_iota(jnp.int32, (NB, NB), 1)
    z_all = jnp.where(row == col, 1.0, 0.0).astype(F32)
    lane = lax.broadcasted_iota(jnp.int32, (1, NB), 1)
    for j in range(0, NB, 4):
        base = (j // 8) * 8
        if a_all.shape[0] != NB - base:
            a_all, z_all = a_all[8:], z_all[8:]
        i, n = j - base, NB - base
        t = [a_all[i + k : i + k + 1, :] for k in range(4)]
        u = [z_all[i + k : i + k + 1, :] for k in range(4)]
        c = [jnp.broadcast_to(a_all[:, j + k : j + k + 1], (n, NB)) for k in range(4)]
        e = {
            (k, m): jnp.broadcast_to(t[k][:, j + m : j + m + 1], (1, NB))
            for k in range(4)
            for m in range(k, 4)
        }
        inv, low = [], {}
        for k in range(4):
            inv.append(1.0 / e[k, k])
            for m in range(k + 1, 4):
                low[m, k] = e[k, m] * inv[k]
            for m in range(k + 1, 4):
                for q in range(m, 4):
                    e[m, q] = e[m, q] - low[m, k] * e[k, q]
        for k in range(4):
            for m in range(k):
                t[k] = t[k] - low[k, m] * t[m]
                u[k] = u[k] - low[k, m] * u[m]
        x, y = [None] * 4, [None] * 4
        for k in reversed(range(4)):
            x[k], y[k] = t[k] * inv[k], u[k] * inv[k]
            for m in range(k + 1, 4):
                x[k] = x[k] - low[m, k] * x[m]
                y[k] = y[k] - low[m, k] * y[m]
        for k in range(4):
            root = lax.rsqrt(e[k, k])
            f_ref[j + k : j + k + 1, :] = jnp.where(lane >= j + k, t[k] * root, 0.0)
            z_ref[j + k : j + k + 1, :] = u[k] * root
        if j + 4 < NB:
            a_all = a_all - ((c[0] * x[0] + c[1] * x[1]) + (c[2] * x[2] + c[3] * x[3]))
            z_all = z_all - ((c[0] * y[0] + c[1] * y[1]) + (c[2] * y[2] + c[3] * y[3]))


def chol_part(info, first, last, pieces=None, places=None, state=None):
    fresh = pieces is not None
    arrays = pieces if fresh else state
    n = arrays[0].shape[1]
    nb = n // NB
    n_in = len(arrays)

    def kernel(info_ref, *refs):
        work, f_out, l_out = refs[n_in : n_in + 3]
        diag, zs, fs = refs[n_in + 3 :]
        if fresh:
            chips = n_in // 2
            for ref, (core, chip) in zip(refs, places):
                h = ref.shape[0]
                off = (info_ref[1] ^ core) * (h * chips) + (info_ref[2] ^ chip) * h
                work[pl.ds(pl.multiple_of(off, 8), h), :] = ref[...]
            f_out[...] = jnp.zeros_like(f_out)
            l_out[...] = jnp.zeros_like(l_out)

        def body(k, carry):
            o = pl.multiple_of(k * NB, NB)
            diag[...] = work[pl.ds(o, NB), pl.ds(o, NB)]
            diag_block(diag, zs, fs)
            for kk in range(first, last):

                @pl.when(k == kk)
                def _():
                    o, e = kk * NB, kk * NB + NB
                    z = zs[...]
                    f_out[o:e, o:e] = fs[...]
                    lk = z
                    if kk > 0:
                        lk = jnp.concatenate([mm(z, l_out[o:e, :o], 1, 0, HIGHEST), z], axis=1)
                    l_out[o:e, :e] = lk
                    if kk < nb - 1:
                        u = mm(z, work[o:e, e:], 1, 0, HIGHEST)
                        f_out[o:e, e:] = u
                        work[e:, e:] -= mm(u, u, 0, 0, HIGHEST)
                        l_out[e:, :e] -= mm(u, lk, 0, 0, HIGHEST)

            return carry

        lax.fori_loop(first, last, body, 0)

    shape = jax.ShapeDtypeStruct((n, n), F32)
    return pl.pallas_call(
        kernel,
        out_shape=(shape, shape, shape),
        in_specs=[SMEM] + [VMEM] * n_in,
        out_specs=(VMEM, VMEM, VMEM),
        scratch_shapes=[pltpu.VMEM((NB, NB), F32)] * 3,
        input_output_aliases={} if fresh else {1: 0, 2: 1, 3: 2},
        compiler_params=vmem_limit(LIMITS[2]),
        cost_estimate=cost((last - first) * 8 * 10**9),
        name="chol_part",
    )(info, *arrays)


def stage(snapshots):
    rows, cols = snapshots.shape

    def kernel(s_ref, h_ref, l_ref):
        for r in range(0, rows, 256):
            h_ref[r : r + 256, :], l_ref[r : r + 256, :] = split(s_ref[r : r + 256, :])

    return pl.pallas_call(
        kernel,
        out_shape=(jax.ShapeDtypeStruct((rows, cols), BF16),) * 2,
        in_specs=[VMEM],
        out_specs=(VMEM, VMEM),
        compiler_params=vmem_limit(LIMITS[0]),
        cost_estimate=cost(10**9),
        name="stage",
    )(snapshots)


def basis(panels, linv):
    rows, n_panels = panels[0].shape[0], len(panels)

    def kernel(*refs):
        p_refs, (l_ref, b_ref, b3, l3) = refs[:n_panels], refs[n_panels:]
        lh, ll = split(l_ref[...])
        l3[:, :PB], l3[:, PB : 2 * PB], l3[:, 2 * PB :] = lh, lh, ll

        def step(i, carry):
            cut = pl.ds(pl.multiple_of(i * 256, 256), 256)
            lh, ll = l3[:, :PB], l3[:, 2 * PB :]
            ph, plow = split(jnp.concatenate([p[cut, :] for p in p_refs], axis=1))
            b = mm(ph, lh, 1, 1) + (mm(ph, ll, 1, 1) + mm(plow, lh, 1, 1))
            b_ref[cut, :] = b
            bh, bl = split(b)
            b3[cut, :PB], b3[cut, PB : 2 * PB], b3[cut, 2 * PB :] = bh, bh, bl
            return carry

        lax.fori_loop(0, rows // 256, step, 0)

    return pl.pallas_call(
        kernel,
        out_shape=(
            jax.ShapeDtypeStruct((rows, PB), F32),
            jax.ShapeDtypeStruct((rows, 3 * PB), BF16),
            jax.ShapeDtypeStruct((PB, 3 * PB), BF16),
        ),
        in_specs=[VMEM] * (n_panels + 1),
        out_specs=(VMEM,) * 3,
        compiler_params=vmem_limit(LIMITS[2]),
        cost_estimate=cost(6 * rows * PB * PB),
        name="basis",
    )(*panels, linv)


def finish(info, snapshots, b, b3, l3, factor, pieces, layout):
    rows, cols = snapshots.shape
    tile = min(TILE, cols)
    n_pieces = len(pieces)
    chips = 1 + max(chip for _, _, chip in layout)

    def kernel(info_ref, s_ref, b_ref, b3_ref, l3_ref, f_ref, *rest):
        m_refs = rest[:n_pieces]
        up_hbm, co_hbm, ms, m3, p3, up, co, sems = rest[n_pieces:]
        copies = []
        for t in range(cols // tile):
            slot, cut = t % 2, pl.ds(t * tile, tile)
            if t >= 2:
                for copy in copies[t - 2]:
                    copy.wait()
            for ref, (base, core, chip) in zip(m_refs, layout):
                h = ref.shape[0]
                off = base + (info_ref[1] ^ core) * (h * chips) + (info_ref[2] ^ chip) * h
                ms[pl.ds(pl.multiple_of(off, 8), h), :] = ref[:, cut]
            mh, ml = split(ms[...])
            m3[:PB, :], m3[PB : 2 * PB, :], m3[2 * PB :, :] = mh, ml, mh
            proj = mm(l3_ref[...], m3[...], 1, 0)
            ph, plow = split(proj)
            p3[:PB, :], p3[PB : 2 * PB, :], p3[2 * PB :, :] = ph, plow, ph
            co[slot] = proj
            up[slot] = s_ref[:, cut] - mm(b3_ref[...], p3[...], 1, 0)
            if t * tile < PB:

                @pl.when(info_ref[0] == 0)
                def _():
                    co[slot] = f_ref[:, cut]
                    up[slot] = b_ref[:, cut]

            pair = (
                pltpu.make_async_copy(up.at[slot], up_hbm.at[:, cut], sems.at[0, slot]),
                pltpu.make_async_copy(co.at[slot], co_hbm.at[:, cut], sems.at[1, slot]),
            )
            for copy in pair:
                copy.start()
            copies.append(pair)
        for pair in copies[-2:]:
            for copy in pair:
                copy.wait()

    return pl.pallas_call(
        kernel,
        out_shape=(
            jax.ShapeDtypeStruct((rows, cols), F32),
            jax.ShapeDtypeStruct((PB, cols), F32),
        ),
        in_specs=[SMEM] + [VMEM] * (5 + n_pieces),
        out_specs=(ANY, ANY),
        scratch_shapes=[
            pltpu.VMEM((PB, tile), F32),
            pltpu.VMEM((3 * PB, tile), BF16),
            pltpu.VMEM((3 * PB, tile), BF16),
            pltpu.VMEM((2, rows, tile), F32),
            pltpu.VMEM((2, PB, tile), F32),
            pltpu.SemaphoreType.DMA((2, 2)),
        ],
        compiler_params=vmem_limit(LIMITS[3]),
        cost_estimate=cost(10**10),
        name="finish",
    )(info, snapshots, b, b3, l3, factor, *pieces)


def panel_dot(info, own, high, low, parts, size, scale):
    rows, width = own.shape
    cols, half = high.shape[1], width // 2
    n_parts = len(parts)
    tile = min(TILE, cols)

    def kernel(info_ref, h_ref, l_ref, own_ref, *rest):
        part_refs = rest[:n_parts]
        send_ref, mine_ref, p_ref, pt, ms = rest[n_parts:]

        @pl.when(info_ref[0] == 0)
        def _():
            p_ref[...] = own_ref[...]

        if n_parts:

            @pl.when(info_ref[0] != 0)
            def _():
                for k, ref in enumerate(part_refs):
                    start = pl.multiple_of(info_ref[3 + k], 8)
                    p_ref[pl.ds(start, size), :] = ref[...]

        for r in range(0, rows, 256):
            ph, plow = split(p_ref[r : r + 256, :])
            pt[:width, r : r + 256], pt[width:, r : r + 256] = ph.T, plow.T

        def step(i, carry):
            cut = pl.ds(pl.multiple_of(i * tile, tile), tile)
            both = mm(pt[...], h_ref[:, cut], 1, 0)
            ms[...] = (both[:width] + (both[width:] + mm(pt[:width, :], l_ref[:, cut], 1, 0))) * scale
            send_ref[:, cut] = ms[pl.ds(pl.multiple_of((1 - info_ref[1]) * half, half), half), :]
            mine_ref[:, cut] = ms[pl.ds(pl.multiple_of(info_ref[1] * half, half), half), :]
            return carry

        lax.fori_loop(0, cols // tile, step, 0)

    out = jax.ShapeDtypeStruct((half, cols), F32)
    return pl.pallas_call(
        kernel,
        out_shape=(out, out, jax.ShapeDtypeStruct((rows, width), F32)),
        in_specs=[SMEM] + [VMEM] * (3 + n_parts),
        out_specs=(VMEM, VMEM, VMEM),
        scratch_shapes=[
            pltpu.VMEM((2 * width, rows), BF16),
            pltpu.VMEM((width, tile), F32),
        ],
        compiler_params=vmem_limit(LIMITS[1]),
        cost_estimate=cost(6 * rows * cols * width),
        name="panel_dot",
    )(info, high, low, own, *parts)


def part_size(rows, parts):
    return -(-rows // (8 * parts)) * 8


def spread_out(x, n):
    rows, parts = x.shape[0], n - 1
    size = part_size(rows, parts)
    got = []
    for k in reversed(range(parts)):
        start = min(k * size, rows - size)
        got.append(lax.ppermute(x[start : start + size], "cols", [(0, k + 1)]))
    return sum(got[1:], got[0])


def spread_round(mine, n):
    got, parts = [mine], n - 1
    for k in range(1, parts):
        pairs = [(1 + i, 1 + (i + k) % parts) for i in range(parts)]
        got.append(lax.ppermute(mine, "cols", pairs))
    return got


def after(x, *others):
    return lax.optimization_barrier((x, others))[0]


def swap(n, k):
    return [(i, i ^ k) for i in range(n)]


def take(a, start, size):
    return lax.dynamic_slice_in_dim(a, start, size, 0)


def join_cores(send, mine, n):
    return mine + lax.ppermute(send, "rows", swap(n, 1))


def scatter_chips(mine, n):
    chips = n // 2
    chip = lax.axis_index("rows") >> 1
    piece = mine.shape[0] // chips
    own = take(mine, chip * piece, piece)
    for k in range(1, chips):
        own = own + lax.ppermute(take(mine, (chip ^ k) * piece, piece), "rows", swap(n, 2 * k))
    return own


def gather_rows(own, n, hold=()):
    got = [own] + [lax.ppermute(own, "rows", swap(n, 2 * k)) for k in range(1, n // 2)]
    other = [lax.ppermute(after(g, hold), "rows", swap(n, 1)) for g in got]
    return got + other, [(0, k) for k in range(n // 2)] + [(1, k) for k in range(n // 2)]


def shards(snapshots):
    rows_dev, cols_dev = snapshots.shape
    n_rows, n_cols = lax.axis_size("rows"), lax.axis_size("cols")
    total_rows = rows_dev * n_rows
    z, index = lax.axis_index("cols"), lax.axis_index("rows")
    core = index & 1
    parts = n_cols - 1
    size = part_size(rows_dev, parts)
    starts = [jnp.minimum(((z - 1 - k) % parts) * size, rows_dev - size) for k in range(parts)]
    info = jnp.stack([z, core, index >> 1] + starts).astype(jnp.int32)
    half = PB // 2
    panel = snapshots[:, :PB]

    dot = lambda got, base: panel_dot(
        info, panel[:, base : base + half], high, low, got, size, 1.0 / total_rows
    )

    mine_a = spread_out(panel[:, :half], n_cols)
    gram = mm(panel, panel, 0, 0, HIGHEST) / total_rows
    joined = join_cores(take(gram, (1 - core) * half, half), take(gram, core * half, half), n_rows)
    high, low = stage(snapshots)
    share = scatter_chips(joined, n_rows)
    far = [lax.ppermute(share, "cols", [(0, k)]) for k in reversed(range(1, n_cols))]
    got_a = spread_round(mine_a, n_cols)
    mine_b = spread_out(after(panel[:, half:], mine_a), n_cols)
    share = jnp.where(z == 0, share, sum(far, jnp.zeros_like(share)))
    grams, places = gather_rows(share, n_rows)

    send, keep, panel_a = dot(after(got_a, far, mine_b, high), 0)
    joined = join_cores(send, keep, n_rows)
    got_b = spread_round(mine_b, n_cols)
    own_a = scatter_chips(joined, n_rows)
    state = chol_part(info, 0, 2, pieces=after(grams, joined, mine_b), places=places)
    pieces_a, where = gather_rows(own_a, n_rows)
    send, keep, panel_b = dot(after(got_b, own_a, state), half)
    joined = join_cores(send, keep, n_rows)
    own_b = scatter_chips(joined, n_rows)
    _, factor, linv = chol_part(info, 2, 4, state=after(state, joined))
    b, b3, l3 = basis([panel_a, panel_b], linv)
    pieces_b, _ = gather_rows(after(own_b, linv), n_rows, (b3,))
    layout = [(base,) + w for base in (0, half) for w in where]
    return finish(info, snapshots, b, b3, l3, factor, pieces_a + pieces_b, layout)


def solution(mesh):
    in_specs = (P("rows", "cols"),)
    out_specs = (P("rows", "cols"), P(None, "cols"))
    return jax.shard_map(shards, mesh=mesh, in_specs=in_specs, out_specs=out_specs, check_vma=False)
```
